512 devices in a mesh: slab: 256 (over z, y, x), col: 2 (over core).
Axes of the slice: x: 4, y: 4, z: 16, core: 2. Of those that a mesh axis runs over, the one named last changes fastest.
Arguments:
- populations: float32 [19, 512, 32, 128], P(None, 'slab', 'col'), may hold values from 0.75 to 1.5
- wall_flags: int32 [512, 32, 128], P('slab', 'col'), may hold values 0 or 1
Outputs:
- image: float32 [4, 128, 512], P(None, 'col', 'slab')
- final_populations: float32 [19, 512, 32, 128], P(None, 'slab', 'col')
The draws below stay inside these ranges and needn't reach their ends.
Inputs may be any that keep to these rules, and one draw needn't show every extreme that they name: `wall_flags`: 1 marks a wall node, 0 a fluid node.
All inputs are finite; a program needn't handle non-finite values. No bound on the sum of `wall_flags` on one device may be relied on, other than what follows from the above.
Results may differ from the reference program's by a relative error of at most 0.00024.
Values sent between devices are 32-bit elements; how exact they have to be, the bound alone decides.
No kernel may reach another device: no remote copies, remote signals or barrier semaphores. Data moves between devices by JAX's collectives and lax.ppermute only.
A program may use at most 64 MiB of HBM per device.

```python
import jax
import jax.numpy as jnp
from jax import lax

PLANES = 2
NX = 128
STEPS = 2
NY = 32
NZ = 512
N_SLAB = 256


def plant(drawn, stream_key, smallest, high):
    place = [jax.random.randint(jax.random.fold_in(stream_key, axis), (), 0, length) for axis, length in enumerate(drawn.shape)]
    main_axis = drawn.shape.index(max(drawn.shape))
    beside = place[:main_axis] + [(place[main_axis] + 1) % drawn.shape[main_axis]] + place[main_axis + 1:]
    return drawn.at[tuple(place)].set(smallest).at[tuple(beside)].set(high)


def shard_levels(stream_key, extent, split, least, high):
    loudness = 1.0
    for axis_at, blocks in split:
        heights = jax.random.uniform(jax.random.fold_in(jax.random.fold_in(stream_key, 6), axis_at), (blocks,), jnp.float32, least / len(split), high / len(split))
        loudness = loudness * jnp.repeat(jnp.exp(heights), extent[axis_at] // blocks).reshape((-1,) + (1,) * (len(extent) - 1 - axis_at))
    return loudness


def setup_inputs(seed: int = 0) -> dict:
    splits = jax.random.split(jax.random.key(seed), 3)
    return {
        "populations": jnp.clip(0.75 + 0.75 * jax.random.uniform(splits[0], (19, NZ, NY, NX), jnp.float32) ** shard_levels(splits[0], (19, NZ, NY, NX), ((1, 256), (2, 2)), -0.2, 0.2), 0.75, 1.5),
        "wall_flags": plant((jax.random.randint(splits[1], (NZ, NY, NX), 0, 8) < 1).astype(jnp.int32), jax.random.fold_in(splits[1], 1), 0, 1),
    }


lattice_dirs = ((0, 0, 0), (0, 0, 1), (1, 0, 1), (-1, 0, 1), (0, 1, 1), (0, -1, 1), (0, 0, -1), (1, 0, -1), (-1, 0, -1), (0, 1, -1), (0, -1, -1), (1, 0, 0), (-1, 0, 0), (0, 1, 0), (0, -1, 0), (1, 1, 0), (-1, -1, 0), (1, -1, 0), (-1, 1, 0))
opposite_dir = tuple(lattice_dirs.index(tuple(-element for element in direction)) for direction in lattice_dirs)
lattice_weights = tuple(1.0 / 3.0 if sum(abs(element) for element in direction) == 0 else (1.0 / 18.0 if sum(abs(element) for element in direction) == 1 else 1.0 / 36.0) for direction in lattice_dirs)
speed_gain = 10000.0
optical = 2.0


def moments(lattice_state):
    vel_table = jnp.asarray(lattice_dirs, dtype=jnp.float32)
    density = jnp.sum(lattice_state, axis=0)
    momentum = jnp.einsum("iv,izyx->vzyx", vel_table, lattice_state, precision=lax.Precision.HIGHEST)
    velocity = momentum / density[None]
    speed_sq = jnp.sum(velocity * velocity, axis=0)
    return density, velocity, speed_sq


def relax(lattice_state, wall_flags):
    density, velocity, speed_sq = moments(lattice_state)
    vel_table = jnp.asarray(lattice_dirs, dtype=jnp.float32)
    weights = jnp.asarray(lattice_weights, dtype=jnp.float32)
    project = jnp.einsum("iv,vzyx->izyx", vel_table, velocity, precision=lax.Precision.HIGHEST)
    balance = weights[:, None, None, None] * density[None] * (1.0 + 3.0 * project + 4.5 * project * project - 1.5 * speed_sq[None])
    bounced = jnp.stack([lattice_state[dir_index] for dir_index in opposite_dir])
    return jnp.where(wall_flags[None] == 1, bounced, balance)


def stream_all(relaxed):
    return jnp.stack([jnp.roll(relaxed[dir_index], (direction[2], direction[1], direction[0]), axis=(0, 1, 2)) for dir_index, direction in enumerate(lattice_dirs)])


def cubic_table(first_row, row_count, coarse, margin, periodic):
    fine_rows = first_row + jnp.arange(row_count, dtype=jnp.int32)
    shifted = fine_rows - 2
    base_cell = shifted // 4
    position = ((shifted % 4).astype(jnp.float32) + 0.5) / 4.0
    third_power = position * position * position
    second_power = position * position
    weight_rows = ((-third_power + 2.0 * second_power - position) / 2.0, (3.0 * third_power - 5.0 * second_power + 2.0) / 2.0, (-3.0 * third_power + 4.0 * second_power + position) / 2.0, (third_power - second_power) / 2.0)
    columns = jnp.arange(coarse, dtype=jnp.int32)
    interp = jnp.zeros((row_count, coarse), jnp.float32)
    for offset, weight_row in zip((-1, 0, 1, 2), weight_rows):
        target = base_cell + offset + margin
        if periodic:
            target = target % coarse
        interp = interp + weight_row[:, None] * (columns[None, :] == target[:, None]).astype(jnp.float32)
    return interp


def upsample(scalar_field, x_table, y_table):
    depth_count = scalar_field.shape[0]
    row_count = scalar_field.shape[1]
    col_count = scalar_field.shape[2]
    along_x = jnp.dot(scalar_field.reshape(depth_count * row_count, col_count), x_table.T, precision=lax.Precision.HIGHEST, preferred_element_type=jnp.float32)
    along_x = along_x.reshape(depth_count, row_count, x_table.shape[0])
    return jnp.einsum("ry,zyx->zrx", y_table, along_x, precision=lax.Precision.HIGHEST)


def slab_light(sample, total_planes):
    squared = sample * sample
    saturation = squared / (1.0 + squared)
    extinction = (optical / total_planes) * saturation
    opacity = -jnp.expm1(-extinction)
    optical_depth = jnp.cumsum(extinction, axis=0) - extinction
    weight = jnp.exp(-optical_depth) * opacity
    colors = jnp.stack([saturation, 1.0 / (1.0 + squared), jnp.exp(-0.5 * (sample - 1.0) * (sample - 1.0))])
    radiance = jnp.sum(weight[None] * colors, axis=1)
    transmit = jnp.exp(-jnp.sum(extinction, axis=0))
    return radiance, transmit


def reference(populations, wall_flags):
    lattice_state = populations
    for repeat in range(STEPS):
        lattice_state = stream_all(relax(lattice_state, wall_flags))
    scalar_field = speed_gain * moments(lattice_state)[2]
    x_table = cubic_table(0, 4 * NX, NX, 0, True)
    y_table = cubic_table(0, 4 * NY, NY, 0, True)
    blocks = scalar_field.reshape(N_SLAB, PLANES, NY, NX)

    def absorb(running, slab_block):
        radiance_sum, transmit_sum = running
        radiance, transmit = slab_light(upsample(slab_block, x_table, y_table), NZ)
        return (radiance_sum + transmit_sum[None] * radiance, transmit_sum * transmit), None

    start_state = (jnp.zeros((3, 4 * NY, 4 * NX), jnp.float32), jnp.ones((4 * NY, 4 * NX), jnp.float32))
    finished, unused = lax.scan(absorb, start_state, blocks)
    image = jnp.concatenate([finished[0], (1.0 - finished[1])[None]], axis=0)
    return image, lattice_state
```

```python
import functools

import jax
import jax.numpy as jnp
import numpy as np
from jax import lax
from jax.experimental import pallas as pl
from jax.experimental.pallas import tpu as pltpu
from jax.sharding import PartitionSpec as P

DIRS = (
    (0, 0, 0),
    (0, 0, 1), (1, 0, 1), (-1, 0, 1), (0, 1, 1), (0, -1, 1),
    (0, 0, -1), (1, 0, -1), (-1, 0, -1), (0, 1, -1), (0, -1, -1),
    (1, 0, 0), (-1, 0, 0), (0, 1, 0), (0, -1, 0),
    (1, 1, 0), (-1, -1, 0), (1, -1, 0), (-1, 1, 0),
)
OPP = tuple(DIRS.index(tuple(-e for e in d)) for d in DIRS)
WEIGHTS = tuple((1.0 / 3.0, 1.0 / 18.0, 1.0 / 36.0)[sum(abs(e) for e in d)] for d in DIRS)
UP = tuple(i for i, d in enumerate(DIRS) if d[2] == 1)
MID = tuple(i for i, d in enumerate(DIRS) if d[2] == 0)
DOWN = tuple(i for i, d in enumerate(DIRS) if d[2] == -1)
SPEED_GAIN = 10000.0
OPTICAL = 2.0

FLAG = len(MID) + 2 * len(UP)
UNITS = FLAG + 1
UP_SLOT = {d: k for k, d in enumerate(MID + UP)}
UP_FAR = {d: len(MID) + len(UP) + k for k, d in enumerate(UP)}
DOWN_SLOT = {d: k for k, d in enumerate(MID + DOWN)}
DOWN_FAR = {d: len(MID) + len(DOWN) + k for k, d in enumerate(DOWN)}

VMEM_BYTES = 12 << 20
HALO = 4


def along(direction, vector):
    total = None
    for element, part in zip(direction, vector):
        if element:
            term = part if element > 0 else -part
            total = term if total is None else total + term
    return total


def add_moments(state):
    density = state[0]
    momentum = [None, None, None]
    for i in range(1, len(DIRS)):
        density = density + state[i]
        for axis, element in enumerate(DIRS[i]):
            if element:
                held = momentum[axis]
                if held is None:
                    momentum[axis] = state[i] if element > 0 else -state[i]
                else:
                    momentum[axis] = held + state[i] if element > 0 else held - state[i]
    return density, momentum


def relax(state, wall, wanted):
    density, momentum = add_moments(state)
    inverse = 1.0 / density
    velocity = [part * inverse for part in momentum]
    speed_sq = velocity[0] * velocity[0] + velocity[1] * velocity[1] + velocity[2] * velocity[2]
    rest = 1.0 - 1.5 * speed_sq
    scaled = {w: w * density for w in set(WEIGHTS)}
    out = {}
    for i, direction in enumerate(DIRS):
        if i > OPP[i] or (i not in wanted and OPP[i] not in wanted):
            continue
        mass = scaled[WEIGHTS[i]]
        if i == 0:
            out[0] = jnp.where(wall, state[0], mass * rest)
            continue
        project = along(direction, velocity)
        even = rest + 4.5 * project * project
        odd = 3.0 * project
        if i in wanted:
            out[i] = jnp.where(wall, state[OPP[i]], mass * (even + odd))
        if OPP[i] in wanted:
            out[OPP[i]] = jnp.where(wall, state[i], mass * (even - odd))
    return out


def edge_kernel(pops_ref, flags_ref, edge_ref):
    lower = lax.broadcasted_iota(jnp.int32, (8, 128), 0) < HALO
    for plane in range(2):
        for i in range(len(DIRS)):
            edge_ref[i, plane] = jnp.where(lower, pops_ref[i, plane, 0:8], pops_ref[i, plane, 8:16])
        flags = jnp.where(lower, flags_ref[plane, 0:8], flags_ref[plane, 8:16])
        edge_ref[len(DIRS), plane] = flags.astype(jnp.float32)


def first_kernel(pops_ref, flags_ref, edge_ref, up_ref, down_ref):
    for plane in range(2):
        for tile in range(3):
            rows = slice(8 * tile, 8 * tile + 8)
            if tile < 2:
                state = [pops_ref[i, plane, rows] for i in range(len(DIRS))]
                flags = flags_ref[plane, rows].astype(jnp.float32)
            else:
                state = [edge_ref[i, plane] for i in range(len(DIRS))]
                flags = edge_ref[len(DIRS), plane]
            out = relax(state, flags > 0.5, range(len(DIRS)))
            near, far_slot, near_slot, far_ref, far_dirs = (
                (down_ref, UP_FAR, DOWN_SLOT, up_ref, UP)
                if plane == 0
                else (up_ref, DOWN_FAR, UP_SLOT, down_ref, DOWN)
            )
            for i, slot in near_slot.items():
                near[slot, rows] = out[i]
            for i in far_dirs:
                far_ref[far_slot[i], rows] = out[i]
            near[FLAG, rows] = flags


def shifted(value, direction):
    cx, cy, _ = direction
    if cy:
        value = pltpu.roll(value, cy % value.shape[0], 0)
    if cx:
        value = pltpu.roll(value, cx % value.shape[1], 1)
    return value


def second_kernel(up_ref, down_ref, below_ref, above_ref, table_ref, final_ref, send_ref, passed_ref, relaxed_ref, spread_ref):
    near = ((below_ref, UP_SLOT), (down_ref, DOWN_SLOT), (up_ref, UP_SLOT), (above_ref, DOWN_SLOT))
    from_below = ((below_ref, UP_FAR), (below_ref, UP_SLOT), (up_ref, UP_FAR), (up_ref, UP_SLOT))
    from_above = ((down_ref, DOWN_SLOT), (down_ref, DOWN_FAR), (above_ref, DOWN_SLOT), (above_ref, DOWN_FAR))
    wanted = (UP, range(len(DIRS)), range(len(DIRS)), DOWN)
    spread_ref[...] = jnp.zeros(spread_ref.shape, jnp.float32)
    for plane in range(4):
        for i, direction in enumerate(DIRS):
            ref, slots = (near, from_below, from_above)[direction[2]][plane]
            passed_ref[plane, i] = shifted(ref[slots[i]], direction)
        for tile in range(3):
            rows = slice(8 * tile, 8 * tile + 8)
            state = [passed_ref[plane, i, rows] for i in range(len(DIRS))]
            out = relax(state, near[plane][0][FLAG, rows] > 0.5, wanted[plane])
            for i in wanted[plane]:
                relaxed_ref[plane, i, rows] = out[i]
    for plane in range(2):
        state = []
        for i, direction in enumerate(DIRS):
            value = shifted(relaxed_ref[plane + 1 - direction[2], i], direction)
            final_ref[i, plane] = value[0:16]
            state.append(value)
        density, momentum = add_moments(state)
        inverse = 1.0 / density
        velocity = [part * inverse for part in momentum]
        scalar = SPEED_GAIN * (velocity[0] * velocity[0] + velocity[1] * velocity[1] + velocity[2] * velocity[2])
        spread_ref[24 * plane : 24 * plane + 24, 0:128] = scalar
        spread_ref[64 + 24 * plane : 64 + 24 * plane + 24, 128:256] = scalar
    send_ref[...] = lax.dot_general(
        table_ref[...],
        spread_ref[...],
        (((1,), (1,)), ((), ())),
        precision=lax.Precision.HIGHEST,
        preferred_element_type=jnp.float32,
    )


def render_kernel(total_planes, got_ref, table_ref, image_ref):
    slabs = got_ref.shape[0]
    groups = slabs // 8
    ordered = jnp.concatenate([got_ref[pl.ds(j, 8, stride=groups), :] for j in range(groups)], axis=0)
    samples = jnp.dot(
        ordered, table_ref[...], precision=lax.Precision.HIGHEST, preferred_element_type=jnp.float32
    )
    depth = jnp.zeros((8, 128), jnp.float32)
    light = [jnp.zeros((8, 128), jnp.float32) for _ in range(3)]
    for j in range(groups):
        for plane in range(2):
            sample = samples[8 * j : 8 * j + 8, 128 * plane : 128 * plane + 128]
            squared = sample * sample
            green = 1.0 / (1.0 + squared)
            saturation = squared * green
            extinction = (OPTICAL / total_planes) * saturation
            opacity = extinction * (
                1.0 - extinction * (0.5 - extinction * (1.0 / 6.0 - extinction * (1.0 / 24.0)))
            )
            blue = jnp.exp(-0.5 * (sample - 1.0) * (sample - 1.0))
            weight = jnp.exp(-depth) * opacity
            light[0] = light[0] + weight * saturation
            light[1] = light[1] + weight * green
            light[2] = light[2] + weight * blue
            depth = depth + extinction
    row = lax.broadcasted_iota(jnp.int32, (8, 128), 0)
    ahead = depth
    for step in (1, 2, 4):
        ahead = ahead + jnp.where(row >= step, pltpu.roll(ahead, step, 0), 0.0)
    through = jnp.exp(depth - ahead)
    sums = [jnp.sum(part * through, axis=0, keepdims=True) for part in light]
    sums.append(1.0 - jnp.exp(-jnp.sum(depth, axis=0, keepdims=True)))
    for channel, value in enumerate(sums):
        image_ref[channel, 0:1, :] = value[:, 0:64]
        image_ref[channel, 1:2, :] = value[:, 64:128]


def cubic_weights(row):
    t = (row % 4 + 0.5) / 4.0
    return (
        (-(t**3) + 2.0 * t**2 - t) / 2.0,
        (3.0 * t**3 - 5.0 * t**2 + 2.0) / 2.0,
        (-3.0 * t**3 + 4.0 * t**2 + t) / 2.0,
        (t**3 - t**2) / 2.0,
    )


def x_table(nodes):
    table = np.zeros((2 * nodes, 2 * nodes), np.float32)
    for fine in range(4 * nodes):
        for offset, weight in zip((-1, 0, 1, 2), cubic_weights(fine - 2)):
            table[fine // 2, (fine % 2) * nodes + ((fine - 2) // 4 + offset) % nodes] += weight
    return table


def y_table(rows):
    held = rows + 2 * HALO
    table = np.zeros((128, 256), np.float32)
    for fine in range(4 * rows):
        for offset, weight in zip((-1, 0, 1, 2), cubic_weights(fine - 2)):
            for column in range(2):
                for plane in range(2):
                    source = 64 * column + held * plane + ((fine - 2) // 4 + offset) % held
                    table[source, 128 * plane + 4 * rows * column + fine] += weight
    return table


def call(kernel, outs, scratch=(), name=None):
    vmem = pl.BlockSpec(memory_space=pltpu.VMEM)

    def run(*operands):
        shapes = [jax.ShapeDtypeStruct(shape, jnp.float32) for shape in outs]
        return pl.pallas_call(
            kernel,
            out_shape=shapes,
            in_specs=[vmem] * len(operands),
            out_specs=[vmem] * len(outs),
            scratch_shapes=[pltpu.VMEM(shape, jnp.float32) for shape in scratch],
            compiler_params=pltpu.CompilerParams(vmem_limit_bytes=VMEM_BYTES),
            name=name,
        )(*operands)

    return run


def body(populations, wall_flags):
    slabs = lax.axis_size("slab")
    dirs, planes, rows, nodes = populations.shape
    held = rows + 2 * HALO
    (edge,) = call(edge_kernel, [(dirs + 1, planes, 8, nodes)], name="edge")(populations, wall_flags)
    edge = lax.ppermute(edge, "col", [(0, 1), (1, 0)])
    message = (UNITS, held, nodes)
    up, down = call(first_kernel, [message, message], name="first")(populations, wall_flags, edge)
    below = lax.ppermute(up, "slab", [(i, (i + 1) % slabs) for i in range(slabs)])
    above = lax.ppermute(down, "slab", [((i + 1) % slabs, i) for i in range(slabs)])
    final, send = call(
        second_kernel,
        [populations.shape, (slabs, 128)],
        scratch=[(4, dirs, held, nodes), (4, dirs, held, nodes), (128, 256)],
        name="second",
    )(up, down, below, above, jnp.asarray(x_table(nodes)))
    got = lax.all_to_all(send, "slab", 0, 0, tiled=True)
    (image,) = call(
        functools.partial(render_kernel, planes * slabs), [(4, 2, 4 * rows)], name="render"
    )(got, jnp.asarray(y_table(rows)))
    return jnp.transpose(image, (0, 2, 1)), final


def solution(mesh):
    return jax.shard_map(
        body,
        mesh=mesh,
        in_specs=(P(None, "slab", "col", None), P("slab", "col", None)),
        out_specs=(P(None, "col", "slab"), P(None, "slab", "col", None)),
        check_vma=False,
    )
```

```python
import functools

import jax
import jax.numpy as jnp
import numpy as np
from jax import lax
from jax.experimental import pallas as pl
from jax.experimental.pallas import tpu as pltpu
from jax.sharding import PartitionSpec as P

DIRS = (
    (0, 0, 0),
    (0, 0, 1), (1, 0, 1), (-1, 0, 1), (0, 1, 1), (0, -1, 1),
    (0, 0, -1), (1, 0, -1), (-1, 0, -1), (0, 1, -1), (0, -1, -1),
    (1, 0, 0), (-1, 0, 0), (0, 1, 0), (0, -1, 0),
    (1, 1, 0), (-1, -1, 0), (1, -1, 0), (-1, 1, 0),
)
OPP = tuple(DIRS.index(tuple(-e for e in d)) for d in DIRS)
WEIGHTS = tuple((1.0 / 3.0, 1.0 / 18.0, 1.0 / 36.0)[sum(abs(e) for e in d)] for d in DIRS)
UP = tuple(i for i, d in enumerate(DIRS) if d[2] == 1)
MID = tuple(i for i, d in enumerate(DIRS) if d[2] == 0)
DOWN = tuple(i for i, d in enumerate(DIRS) if d[2] == -1)
SPEED_GAIN = 10000.0
OPTICAL = 2.0

FLAG = len(MID) + 2 * len(UP)
UNITS = FLAG + 1
UP_SLOT = {d: k for k, d in enumerate(MID + UP)}
UP_FAR = {d: len(MID) + len(UP) + k for k, d in enumerate(UP)}
DOWN_SLOT = {d: k for k, d in enumerate(MID + DOWN)}
DOWN_FAR = {d: len(MID) + len(DOWN) + k for k, d in enumerate(DOWN)}

VMEM_BYTES = 12 << 20
HALO = 4


def along(direction, vector):
    total = None
    for element, part in zip(direction, vector):
        if element:
            term = part if element > 0 else -part
            total = term if total is None else total + term
    return total


def add_moments(state):
    density = state[0]
    momentum = [None, None, None]
    for i in range(1, len(DIRS)):
        density = density + state[i]
        for axis, element in enumerate(DIRS[i]):
            if element:
                held = momentum[axis]
                if held is None:
                    momentum[axis] = state[i] if element > 0 else -state[i]
                else:
                    momentum[axis] = held + state[i] if element > 0 else held - state[i]
    return density, momentum


def relax(state, wall, wanted):
    density, momentum = add_moments(state)
    inverse = 1.0 / density
    velocity = [part * inverse for part in momentum]
    speed_sq = velocity[0] * velocity[0] + velocity[1] * velocity[1] + velocity[2] * velocity[2]
    rest = 1.0 - 1.5 * speed_sq
    scaled = {w: w * density for w in set(WEIGHTS)}
    out = {}
    for i, direction in enumerate(DIRS):
        if i > OPP[i] or (i not in wanted and OPP[i] not in wanted):
            continue
        mass = scaled[WEIGHTS[i]]
        if i == 0:
            out[0] = jnp.where(wall, state[0], mass * rest)
            continue
        project = along(direction, velocity)
        even = rest + 4.5 * project * project
        odd = 3.0 * project
        if i in wanted:
            out[i] = jnp.where(wall, state[OPP[i]], mass * (even + odd))
        if OPP[i] in wanted:
            out[OPP[i]] = jnp.where(wall, state[i], mass * (even - odd))
    return out


def edge_kernel(pops_hbm, flags_hbm, edge_ref, pops_ref, flags_ref, sems):
    copies = [
        pltpu.make_async_copy(pops_hbm, pops_ref, sems.at[0]),
        pltpu.make_async_copy(flags_hbm, flags_ref, sems.at[1]),
    ]
    for copy in copies:
        copy.start()
    for copy in copies:
        copy.wait()
    lower = lax.broadcasted_iota(jnp.int32, (8, 128), 0) < HALO
    for plane in range(2):
        for i in range(len(DIRS)):
            edge_ref[i, plane] = jnp.where(lower, pops_ref[i, plane, 0:8], pops_ref[i, plane, 8:16])
        flags = jnp.where(lower, flags_ref[plane, 0:8], flags_ref[plane, 8:16])
        edge_ref[len(DIRS), plane] = flags.astype(jnp.float32)


def first_kernel(odd_ref, pops_ref, flags_ref, edge_ref, up_ref, down_ref, inner_ref, outer_ref):
    for plane in range(2):
        for tile in range(3):
            rows = slice(8 * tile, 8 * tile + 8)
            if tile < 2:
                state = [pops_ref[i, plane, rows] for i in range(len(DIRS))]
                flags = flags_ref[plane, rows].astype(jnp.float32)
            else:
                state = [edge_ref[i, plane] for i in range(len(DIRS))]
                flags = edge_ref[len(DIRS), plane]
            out = relax(state, flags > 0.5, range(len(DIRS)))
            near, far_slot, near_slot, far_ref, far_dirs = (
                (down_ref, UP_FAR, DOWN_SLOT, up_ref, UP)
                if plane == 0
                else (up_ref, DOWN_FAR, UP_SLOT, down_ref, DOWN)
            )
            for i, slot in near_slot.items():
                near[slot, rows] = out[i]
            for i in far_dirs:
                far_ref[far_slot[i], rows] = out[i]
            near[FLAG, rows] = flags
    odd = jnp.full(up_ref.shape[1:], odd_ref[0]) == 1
    for slot in range(UNITS):
        up, down = up_ref[slot], down_ref[slot]
        inner_ref[slot] = jnp.where(odd, down, up)
        outer_ref[slot] = jnp.where(odd, up, down)


def shifted(value, direction):
    cx, cy, _ = direction
    if cy:
        value = pltpu.roll(value, cy % value.shape[0], 0)
    if cx:
        value = pltpu.roll(value, cx % value.shape[1], 1)
    return value


def second_kernel(
    odd_ref, up_ref, down_ref, inner_ref, outer_ref, table_ref,
    final_ref, send_ref,
    below_ref, above_ref, passed_ref, relaxed_ref, spread_ref,
):
    odd = jnp.full(up_ref.shape[1:], odd_ref[0]) == 1
    for slot in range(UNITS):
        inner, outer = inner_ref[slot], outer_ref[slot]
        below_ref[slot] = jnp.where(odd, inner, outer)
        above_ref[slot] = jnp.where(odd, outer, inner)
    near = ((below_ref, UP_SLOT), (down_ref, DOWN_SLOT), (up_ref, UP_SLOT), (above_ref, DOWN_SLOT))
    from_below = ((below_ref, UP_FAR), (below_ref, UP_SLOT), (up_ref, UP_FAR), (up_ref, UP_SLOT))
    from_above = ((down_ref, DOWN_SLOT), (down_ref, DOWN_FAR), (above_ref, DOWN_SLOT), (above_ref, DOWN_FAR))
    wanted = (UP, range(len(DIRS)), range(len(DIRS)), DOWN)
    spread_ref[...] = jnp.zeros(spread_ref.shape, jnp.float32)
    for plane in range(4):
        for i, direction in enumerate(DIRS):
            ref, slots = (near, from_below, from_above)[direction[2]][plane]
            passed_ref[plane, i] = shifted(ref[slots[i]], direction)
        for tile in range(3):
            rows = slice(8 * tile, 8 * tile + 8)
            state = [passed_ref[plane, i, rows] for i in range(len(DIRS))]
            out = relax(state, near[plane][0][FLAG, rows] > 0.5, wanted[plane])
            for i in wanted[plane]:
                relaxed_ref[plane, i, rows] = out[i]
    for plane in range(2):
        state = []
        for i, direction in enumerate(DIRS):
            value = shifted(relaxed_ref[plane + 1 - direction[2], i], direction)
            final_ref[i, plane] = value[0:16]
            state.append(value)
        density, momentum = add_moments(state)
        inverse = 1.0 / density
        velocity = [part * inverse for part in momentum]
        scalar = SPEED_GAIN * (velocity[0] * velocity[0] + velocity[1] * velocity[1] + velocity[2] * velocity[2])
        spread_ref[24 * plane : 24 * plane + 24, 0:128] = scalar
        spread_ref[64 + 24 * plane : 64 + 24 * plane + 24, 128:256] = scalar
    send_ref[...] = lax.dot_general(
        table_ref[...],
        spread_ref[...],
        (((1,), (1,)), ((), ())),
        precision=lax.Precision.HIGHEST,
        preferred_element_type=jnp.float32,
    )


def render_kernel(total_planes, got_ref, table_ref, image_ref):
    slabs = got_ref.shape[0]
    groups = slabs // 8
    ordered = jnp.concatenate([got_ref[pl.ds(j, 8, stride=groups), :] for j in range(groups)], axis=0)
    samples = jnp.dot(
        ordered, table_ref[...], precision=lax.Precision.HIGHEST, preferred_element_type=jnp.float32
    )
    depth = jnp.zeros((8, 128), jnp.float32)
    light = [jnp.zeros((8, 128), jnp.float32) for _ in range(3)]
    for j in range(groups):
        for plane in range(2):
            sample = samples[8 * j : 8 * j + 8, 128 * plane : 128 * plane + 128]
            squared = sample * sample
            green = 1.0 / (1.0 + squared)
            saturation = squared * green
            extinction = (OPTICAL / total_planes) * saturation
            opacity = extinction * (
                1.0 - extinction * (0.5 - extinction * (1.0 / 6.0 - extinction * (1.0 / 24.0)))
            )
            blue = jnp.exp(-0.5 * (sample - 1.0) * (sample - 1.0))
            weight = jnp.exp(-depth) * opacity
            light[0] = light[0] + weight * saturation
            light[1] = light[1] + weight * green
            light[2] = light[2] + weight * blue
            depth = depth + extinction
    row = lax.broadcasted_iota(jnp.int32, (8, 128), 0)
    ahead = depth
    for step in (1, 2, 4):
        ahead = ahead + jnp.where(row >= step, pltpu.roll(ahead, step, 0), 0.0)
    through = jnp.exp(depth - ahead)
    sums = [jnp.sum(part * through, axis=0, keepdims=True) for part in light]
    sums.append(1.0 - jnp.exp(-jnp.sum(depth, axis=0, keepdims=True)))
    for channel, value in enumerate(sums):
        image_ref[channel, 0:1, :] = value[:, 0:64]
        image_ref[channel, 1:2, :] = value[:, 64:128]


def cubic_weights(row):
    t = (row % 4 + 0.5) / 4.0
    return (
        (-(t**3) + 2.0 * t**2 - t) / 2.0,
        (3.0 * t**3 - 5.0 * t**2 + 2.0) / 2.0,
        (-3.0 * t**3 + 4.0 * t**2 + t) / 2.0,
        (t**3 - t**2) / 2.0,
    )


def x_table(nodes):
    table = np.zeros((2 * nodes, 2 * nodes), np.float32)
    for fine in range(4 * nodes):
        for offset, weight in zip((-1, 0, 1, 2), cubic_weights(fine - 2)):
            table[fine // 2, (fine % 2) * nodes + ((fine - 2) // 4 + offset) % nodes] += weight
    return table


def y_table(rows):
    held = rows + 2 * HALO
    table = np.zeros((128, 256), np.float32)
    for fine in range(4 * rows):
        for offset, weight in zip((-1, 0, 1, 2), cubic_weights(fine - 2)):
            for column in range(2):
                for plane in range(2):
                    source = 64 * column + held * plane + ((fine - 2) // 4 + offset) % held
                    table[source, 128 * plane + 4 * rows * column + fine] += weight
    return table


def call(kernel, outs, scratch=(), spaces=None):
    vmem = pl.BlockSpec(memory_space=pltpu.VMEM)

    def run(*operands):
        shapes = [jax.ShapeDtypeStruct(shape, jnp.float32) for shape in outs]
        return pl.pallas_call(
            kernel,
            out_shape=shapes,
            in_specs=[pl.BlockSpec(memory_space=space) for space in spaces] if spaces else [vmem] * len(operands),
            out_specs=[vmem] * len(outs),
            scratch_shapes=[pltpu.VMEM(part, jnp.float32) if isinstance(part, tuple) else part for part in scratch],
            compiler_params=pltpu.CompilerParams(vmem_limit_bytes=VMEM_BYTES),
        )(*operands)

    return run


def body(populations, wall_flags):
    slabs = lax.axis_size("slab")
    dirs, planes, rows, nodes = populations.shape
    held = rows + 2 * HALO
    (edge,) = call(
        edge_kernel,
        [(dirs + 1, planes, 8, nodes)],
        scratch=[
            populations.shape,
            pltpu.VMEM(wall_flags.shape, jnp.int32),
            pltpu.SemaphoreType.DMA((2,)),
        ],
        spaces=[pltpu.HBM] * 2,
    )(*(pltpu.with_memory_space_constraint(part, pltpu.HBM) for part in (populations, wall_flags)))
    edge = lax.ppermute(edge, "col", [(0, 1), (1, 0)])
    odd = (lax.axis_index("slab") % 2).astype(jnp.int32).reshape(1)
    message = (UNITS, held, nodes)
    up, down, inner, outer = call(
        first_kernel, [message] * 4, spaces=[pltpu.SMEM] + [pltpu.VMEM] * 3
    )(odd, populations, wall_flags, edge)
    outer = lax.ppermute(outer, "slab", [(i, (i + (1 if i % 2 else -1)) % slabs) for i in range(slabs)])
    inner = lax.ppermute(inner, "slab", [(i, i ^ 1) for i in range(slabs)])
    final, send = call(
        second_kernel,
        [populations.shape, (slabs, 128)],
        scratch=[message, message, (4, dirs, held, nodes), (4, dirs, held, nodes), (128, 256)],
        spaces=[pltpu.SMEM] + [pltpu.VMEM] * 5,
    )(odd, up, down, inner, outer, jnp.asarray(x_table(nodes)))
    got = lax.all_to_all(send, "slab", 0, 0, tiled=True)
    (image,) = call(
        functools.partial(render_kernel, planes * slabs), [(4, 2, 4 * rows)]
    )(got, jnp.asarray(y_table(rows)))
    return jnp.transpose(image, (0, 2, 1)), final


def solution(mesh):
    return jax.shard_map(
        body,
        mesh=mesh,
        in_specs=(P(None, "slab", "col", None), P("slab", "col", None)),
        out_specs=(P(None, "col", "slab"), P(None, "slab", "col", None)),
        check_vma=False,
    )
```

```python
import functools

import jax
import jax.numpy as jnp
import numpy as np
from jax import lax
from jax.experimental import pallas as pl
from jax.experimental.pallas import tpu as pltpu
from jax.sharding import PartitionSpec as P

DIRS = (
    (0, 0, 0),
    (0, 0, 1), (1, 0, 1), (-1, 0, 1), (0, 1, 1), (0, -1, 1),
    (0, 0, -1), (1, 0, -1), (-1, 0, -1), (0, 1, -1), (0, -1, -1),
    (1, 0, 0), (-1, 0, 0), (0, 1, 0), (0, -1, 0),
    (1, 1, 0), (-1, -1, 0), (1, -1, 0), (-1, 1, 0),
)
OPP = tuple(DIRS.index(tuple(-e for e in d)) for d in DIRS)
WEIGHTS = tuple((1.0 / 3.0, 1.0 / 18.0, 1.0 / 36.0)[sum(abs(e) for e in d)] for d in DIRS)
UP = tuple(i for i, d in enumerate(DIRS) if d[2] == 1)
MID = tuple(i for i, d in enumerate(DIRS) if d[2] == 0)
DOWN = tuple(i for i, d in enumerate(DIRS) if d[2] == -1)
SPEED_GAIN = 10000.0
OPTICAL = 2.0

MOMENTS = len(UP)
FLAG = MOMENTS + 4
UNITS = FLAG + 1
UP_SLOT = {d: k for k, d in enumerate(UP)}
DOWN_SLOT = {d: k for k, d in enumerate(DOWN)}

VMEM_BYTES = 12 << 20
HALO = 4


def along(direction, vector):
    total = None
    for element, part in zip(direction, vector):
        if element:
            term = part if element > 0 else -part
            total = term if total is None else total + term
    return total


def add_moments(total, state):
    total = list(total) if total else [None] * 4
    for i, value in state.items():
        for part, element in enumerate((1,) + DIRS[i]):
            if element:
                held = total[part]
                if held is None:
                    total[part] = value if element > 0 else -value
                else:
                    total[part] = held + value if element > 0 else held - value
    return total


def relax(total, state, wall, wanted):
    density = total[0]
    inverse = 1.0 / density
    velocity = [part * inverse for part in total[1:]]
    speed_sq = velocity[0] * velocity[0] + velocity[1] * velocity[1] + velocity[2] * velocity[2]
    rest = 1.0 - 1.5 * speed_sq
    scaled = {w: w * density for w in sorted(set(WEIGHTS))}
    out = {}
    for i, direction in enumerate(DIRS):
        if i > OPP[i] or (i not in wanted and OPP[i] not in wanted):
            continue
        mass = scaled[WEIGHTS[i]]
        if i == 0:
            out[0] = jnp.where(wall, state[0], mass * rest)
            continue
        project = along(direction, velocity)
        even = rest + 4.5 * project * project
        odd = 3.0 * project
        if i in wanted:
            out[i] = jnp.where(wall, state[OPP[i]], mass * (even + odd))
        if OPP[i] in wanted:
            out[OPP[i]] = jnp.where(wall, state[i], mass * (even - odd))
    return out


def edge_kernel(pops_hbm, flags_hbm, edge_ref, pops_ref, flags_ref, sems):
    copies = [
        pltpu.make_async_copy(pops_hbm, pops_ref, sems.at[0]),
        pltpu.make_async_copy(flags_hbm, flags_ref, sems.at[1]),
    ]
    for copy in copies:
        copy.start()
    for copy in copies:
        copy.wait()
    lower = lax.broadcasted_iota(jnp.int32, (8, 128), 0) < HALO
    for plane in range(2):
        for i in range(len(DIRS)):
            edge_ref[i, plane] = jnp.where(lower, pops_ref[i, plane, 0:8], pops_ref[i, plane, 8:16])
        flags = jnp.where(lower, flags_ref[plane, 0:8], flags_ref[plane, 8:16])
        edge_ref[len(DIRS), plane] = flags.astype(jnp.float32)


def first_kernel(
    odd_ref, pops_ref, flags_ref, edge_ref,
    passed_ref, up_ref, down_ref, inner_ref, outer_ref,
    relaxed_ref,
):
    for plane, near in ((0, down_ref), (1, up_ref)):
        for tile in range(3):
            rows = slice(8 * tile, 8 * tile + 8)
            if tile < 2:
                state = {i: pops_ref[i, plane, rows] for i in range(len(DIRS))}
                flags = flags_ref[plane, rows].astype(jnp.float32)
            else:
                state = {i: edge_ref[i, plane] for i in range(len(DIRS))}
                flags = edge_ref[len(DIRS), plane]
            out = relax(add_moments(None, state), state, flags > 0.5, range(len(DIRS)))
            for i, value in out.items():
                relaxed_ref[plane, i, rows] = value
            near[FLAG, rows] = flags
    for plane, near, slots, inward in ((0, down_ref, DOWN_SLOT, DOWN), (1, up_ref, UP_SLOT, UP)):
        total = None
        for i in MID + inward:
            value = shifted(relaxed_ref[plane if i in MID else 1 - plane, i], DIRS[i])
            passed_ref[plane, i] = value
            total = add_moments(total, {i: value})
        for part, value in enumerate(total):
            near[MOMENTS + part] = value
        for i, slot in slots.items():
            near[slot] = shifted(relaxed_ref[plane, i], DIRS[i])
    odd = jnp.full(up_ref.shape[1:], odd_ref[0]) == 1
    for slot in range(UNITS):
        up, down = up_ref[slot], down_ref[slot]
        inner_ref[slot] = jnp.where(odd, down, up)
        outer_ref[slot] = jnp.where(odd, up, down)


def shifted(value, direction):
    cx, cy, _ = direction
    if cy:
        value = pltpu.roll(value, cy % value.shape[0], 0)
    if cx:
        value = pltpu.roll(value, cx % value.shape[1], 1)
    return value


def second_kernel(
    odd_ref, passed_ref, up_ref, down_ref, inner_ref, outer_ref, table_ref,
    final_ref, send_ref,
    below_ref, above_ref, relaxed_ref, spread_ref,
):
    odd = jnp.full(up_ref.shape[1:], odd_ref[0]) == 1
    for slot in range(UNITS):
        inner, outer = inner_ref[slot], outer_ref[slot]
        below_ref[slot] = jnp.where(odd, inner, outer)
        above_ref[slot] = jnp.where(odd, outer, inner)
    spread_ref[...] = jnp.zeros(spread_ref.shape, jnp.float32)
    sides = (
        (below_ref, down_ref, DOWN_SLOT, UP),
        (down_ref, below_ref, UP_SLOT, range(len(DIRS))),
        (up_ref, above_ref, DOWN_SLOT, range(len(DIRS))),
        (above_ref, up_ref, UP_SLOT, DOWN),
    )
    for plane, (near, other, slots, wanted) in enumerate(sides):
        for tile in range(3):
            rows = slice(8 * tile, 8 * tile + 8)
            state = {i: other[slot, rows] for i, slot in slots.items()}
            total = add_moments([near[MOMENTS + part, rows] for part in range(4)], state)
            if plane in (1, 2):
                state.update({i: passed_ref[plane - 1, i, rows] for i in range(len(DIRS)) if i not in slots})
            out = relax(total, state, near[FLAG, rows] > 0.5, wanted)
            for i in wanted:
                relaxed_ref[plane, i, rows] = out[i]
    for plane in range(2):
        total = None
        for i, direction in enumerate(DIRS):
            value = shifted(relaxed_ref[plane + 1 - direction[2], i], direction)
            final_ref[i, plane] = value[0:16]
            total = add_moments(total, {i: value})
        inverse = 1.0 / total[0]
        velocity = [part * inverse for part in total[1:]]
        scalar = SPEED_GAIN * (velocity[0] * velocity[0] + velocity[1] * velocity[1] + velocity[2] * velocity[2])
        spread_ref[24 * plane : 24 * plane + 24, 0:128] = scalar
        spread_ref[64 + 24 * plane : 64 + 24 * plane + 24, 128:256] = scalar
    send_ref[...] = lax.dot_general(
        table_ref[...],
        spread_ref[...],
        (((1,), (1,)), ((), ())),
        precision=lax.Precision.HIGHEST,
        preferred_element_type=jnp.float32,
    )


def render_kernel(total_planes, got_ref, table_ref, image_ref):
    slabs = got_ref.shape[0]
    groups = slabs // 8
    ordered = jnp.concatenate([got_ref[pl.ds(j, 8, stride=groups), :] for j in range(groups)], axis=0)
    samples = jnp.dot(
        ordered, table_ref[...], precision=lax.Precision.HIGHEST, preferred_element_type=jnp.float32
    )
    depth = jnp.zeros((8, 128), jnp.float32)
    light = [jnp.zeros((8, 128), jnp.float32) for _ in range(3)]
    for j in range(groups):
        for plane in range(2):
            sample = samples[8 * j : 8 * j + 8, 128 * plane : 128 * plane + 128]
            squared = sample * sample
            green = 1.0 / (1.0 + squared)
            saturation = squared * green
            extinction = (OPTICAL / total_planes) * saturation
            opacity = extinction * (
                1.0 - extinction * (0.5 - extinction * (1.0 / 6.0 - extinction * (1.0 / 24.0)))
            )
            blue = jnp.exp(-0.5 * (sample - 1.0) * (sample - 1.0))
            weight = jnp.exp(-depth) * opacity
            light[0] = light[0] + weight * saturation
            light[1] = light[1] + weight * green
            light[2] = light[2] + weight * blue
            depth = depth + extinction
    row = lax.broadcasted_iota(jnp.int32, (8, 128), 0)
    ahead = depth
    for step in (1, 2, 4):
        ahead = ahead + jnp.where(row >= step, pltpu.roll(ahead, step, 0), 0.0)
    through = jnp.exp(depth - ahead)
    sums = [jnp.sum(part * through, axis=0, keepdims=True) for part in light]
    sums.append(1.0 - jnp.exp(-jnp.sum(depth, axis=0, keepdims=True)))
    for channel, value in enumerate(sums):
        image_ref[channel, 0:1, :] = value[:, 0:64]
        image_ref[channel, 1:2, :] = value[:, 64:128]


def cubic_weights(row):
    t = (row % 4 + 0.5) / 4.0
    return (
        (-(t**3) + 2.0 * t**2 - t) / 2.0,
        (3.0 * t**3 - 5.0 * t**2 + 2.0) / 2.0,
        (-3.0 * t**3 + 4.0 * t**2 + t) / 2.0,
        (t**3 - t**2) / 2.0,
    )


def x_table(nodes):
    table = np.zeros((2 * nodes, 2 * nodes), np.float32)
    for fine in range(4 * nodes):
        for offset, weight in zip((-1, 0, 1, 2), cubic_weights(fine - 2)):
            table[fine // 2, (fine % 2) * nodes + ((fine - 2) // 4 + offset) % nodes] += weight
    return table


def y_table(rows):
    held = rows + 2 * HALO
    table = np.zeros((128, 256), np.float32)
    for fine in range(4 * rows):
        for offset, weight in zip((-1, 0, 1, 2), cubic_weights(fine - 2)):
            for column in range(2):
                for plane in range(2):
                    source = 64 * column + held * plane + ((fine - 2) // 4 + offset) % held
                    table[source, 128 * plane + 4 * rows * column + fine] += weight
    return table


def call(kernel, outs, scratch=(), spaces=None):
    vmem = pl.BlockSpec(memory_space=pltpu.VMEM)

    def run(*operands):
        shapes = [jax.ShapeDtypeStruct(shape, jnp.float32) for shape in outs]
        return pl.pallas_call(
            kernel,
            out_shape=shapes,
            in_specs=[pl.BlockSpec(memory_space=space) for space in spaces] if spaces else [vmem] * len(operands),
            out_specs=[vmem] * len(outs),
            scratch_shapes=[pltpu.VMEM(part, jnp.float32) if isinstance(part, tuple) else part for part in scratch],
            compiler_params=pltpu.CompilerParams(vmem_limit_bytes=VMEM_BYTES),
        )(*operands)

    return run


def body(populations, wall_flags):
    slabs = lax.axis_size("slab")
    dirs, planes, rows, nodes = populations.shape
    held = rows + 2 * HALO
    (edge,) = call(
        edge_kernel,
        [(dirs + 1, planes, 8, nodes)],
        scratch=[
            populations.shape,
            pltpu.VMEM(wall_flags.shape, jnp.int32),
            pltpu.SemaphoreType.DMA((2,)),
        ],
        spaces=[pltpu.HBM] * 2,
    )(*(pltpu.with_memory_space_constraint(part, pltpu.HBM) for part in (populations, wall_flags)))
    edge = lax.ppermute(edge, "col", [(0, 1), (1, 0)])
    odd = (lax.axis_index("slab") % 2).astype(jnp.int32).reshape(1)
    message = (UNITS, held, nodes)
    lattice = (2, dirs, held, nodes)
    passed, up, down, inner, outer = call(
        first_kernel, [lattice] + [message] * 4, scratch=[lattice], spaces=[pltpu.SMEM] + [pltpu.VMEM] * 3
    )(odd, populations, wall_flags, edge)
    outer = lax.ppermute(outer, "slab", [(i, (i + (1 if i % 2 else -1)) % slabs) for i in range(slabs)])
    inner = lax.ppermute(inner, "slab", [(i, i ^ 1) for i in range(slabs)])
    final, send = call(
        second_kernel,
        [populations.shape, (slabs, 128)],
        scratch=[message, message, (4, dirs, held, nodes), (128, 256)],
        spaces=[pltpu.SMEM] + [pltpu.VMEM] * 6,
    )(odd, passed, up, down, inner, outer, jnp.asarray(x_table(nodes)))
    got = lax.all_to_all(send, "slab", 0, 0, tiled=True)
    (image,) = call(
        functools.partial(render_kernel, planes * slabs), [(4, 2, 4 * rows)]
    )(got, jnp.asarray(y_table(rows)))
    return jnp.transpose(image, (0, 2, 1)), final


def solution(mesh):
    return jax.shard_map(
        body,
        mesh=mesh,
        in_specs=(P(None, "slab", "col", None), P("slab", "col", None)),
        out_specs=(P(None, "col", "slab"), P(None, "slab", "col", None)),
        check_vma=False,
    )
```

```python
import functools

import jax
import jax.numpy as jnp
import numpy as np
from jax import lax
from jax.experimental import pallas as pl
from jax.experimental.pallas import tpu as pltpu
from jax.sharding import PartitionSpec as P

DIRS = (
    (0, 0, 0),
    (0, 0, 1), (1, 0, 1), (-1, 0, 1), (0, 1, 1), (0, -1, 1),
    (0, 0, -1), (1, 0, -1), (-1, 0, -1), (0, 1, -1), (0, -1, -1),
    (1, 0, 0), (-1, 0, 0), (0, 1, 0), (0, -1, 0),
    (1, 1, 0), (-1, -1, 0), (1, -1, 0), (-1, 1, 0),
)
OPP = tuple(DIRS.index(tuple(-e for e in d)) for d in DIRS)
WEIGHTS = tuple((1.0 / 3.0, 1.0 / 18.0, 1.0 / 36.0)[sum(abs(e) for e in d)] for d in DIRS)
UP = tuple(i for i, d in enumerate(DIRS) if d[2] == 1)
MID = tuple(i for i, d in enumerate(DIRS) if d[2] == 0)
DOWN = tuple(i for i, d in enumerate(DIRS) if d[2] == -1)
SPEED_GAIN = 10000.0
OPTICAL = 2.0

MOMENTS = len(UP)
FLAG = MOMENTS + 4
UNITS = FLAG + 1
UP_SLOT = {d: k for k, d in enumerate(UP)}
DOWN_SLOT = {d: k for k, d in enumerate(DOWN)}

VMEM_BYTES = 12 << 20
GROUP = 16
HALO = 4


def along(direction, vector):
    total = None
    for element, part in zip(direction, vector):
        if element:
            term = part if element > 0 else -part
            total = term if total is None else total + term
    return total


def add_moments(total, state):
    total = list(total) if total else [None] * 4
    for i, value in state.items():
        for part, element in enumerate((1,) + DIRS[i]):
            if element:
                held = total[part]
                if held is None:
                    total[part] = value if element > 0 else -value
                else:
                    total[part] = held + value if element > 0 else held - value
    return total


def relax(total, state, wall, wanted):
    density = total[0]
    inverse = 1.0 / density
    velocity = [part * inverse for part in total[1:]]
    speed_sq = velocity[0] * velocity[0] + velocity[1] * velocity[1] + velocity[2] * velocity[2]
    rest = 1.0 - 1.5 * speed_sq
    scaled = {w: w * density for w in sorted(set(WEIGHTS))}
    out = {}
    for i, direction in enumerate(DIRS):
        if i > OPP[i] or (i not in wanted and OPP[i] not in wanted):
            continue
        mass = scaled[WEIGHTS[i]]
        if i == 0:
            out[0] = jnp.where(wall, state[0], mass * rest)
            continue
        project = along(direction, velocity)
        even = rest + 4.5 * project * project
        odd = 3.0 * project
        if i in wanted:
            out[i] = jnp.where(wall, state[OPP[i]], mass * (even + odd))
        if OPP[i] in wanted:
            out[OPP[i]] = jnp.where(wall, state[i], mass * (even - odd))
    return out


def edge_kernel(pops_hbm, flags_hbm, edge_ref, pops_ref, flags_ref, sems):
    copies = [
        pltpu.make_async_copy(pops_hbm, pops_ref, sems.at[0]),
        pltpu.make_async_copy(flags_hbm, flags_ref, sems.at[1]),
    ]
    for copy in copies:
        copy.start()
    for copy in copies:
        copy.wait()
    lower = lax.broadcasted_iota(jnp.int32, (8, 128), 0) < HALO
    for plane in range(2):
        for i in range(len(DIRS)):
            edge_ref[i, plane] = jnp.where(lower, pops_ref[i, plane, 0:8], pops_ref[i, plane, 8:16])
        flags = jnp.where(lower, flags_ref[plane, 0:8], flags_ref[plane, 8:16])
        edge_ref[len(DIRS), plane] = flags.astype(jnp.float32)


def first_kernel(
    odd_ref, pops_ref, flags_ref, edge_ref,
    passed_ref, up_ref, down_ref, inner_ref, outer_ref,
    relaxed_ref,
):
    for plane, near in ((0, down_ref), (1, up_ref)):
        for tile in range(3):
            rows = slice(8 * tile, 8 * tile + 8)
            if tile < 2:
                state = {i: pops_ref[i, plane, rows] for i in range(len(DIRS))}
                flags = flags_ref[plane, rows].astype(jnp.float32)
            else:
                state = {i: edge_ref[i, plane] for i in range(len(DIRS))}
                flags = edge_ref[len(DIRS), plane]
            out = relax(add_moments(None, state), state, flags > 0.5, range(len(DIRS)))
            for i, value in out.items():
                relaxed_ref[plane, i, rows] = value
            near[FLAG, rows] = flags
    for plane, near, slots, inward in ((0, down_ref, DOWN_SLOT, DOWN), (1, up_ref, UP_SLOT, UP)):
        total = None
        for i in MID + inward:
            value = shifted(relaxed_ref[plane if i in MID else 1 - plane, i], DIRS[i])
            passed_ref[plane, i] = value
            total = add_moments(total, {i: value})
        for part, value in enumerate(total):
            near[MOMENTS + part] = value
        for i, slot in slots.items():
            near[slot] = shifted(relaxed_ref[plane, i], DIRS[i])
    odd = jnp.full(up_ref.shape[1:], odd_ref[0]) == 1
    for slot in range(UNITS):
        up, down = up_ref[slot], down_ref[slot]
        inner_ref[slot] = jnp.where(odd, down, up)
        outer_ref[slot] = jnp.where(odd, up, down)


def shifted(value, direction):
    cx, cy, _ = direction
    if cy:
        value = pltpu.roll(value, cy % value.shape[0], 0)
    if cx:
        value = pltpu.roll(value, cx % value.shape[1], 1)
    return value


def second_kernel(
    odd_ref, passed_ref, up_ref, down_ref, inner_ref, outer_ref, table_ref,
    final_ref, send_ref,
    below_ref, above_ref, relaxed_ref, spread_ref,
):
    odd = jnp.full(up_ref.shape[1:], odd_ref[0]) == 1
    for slot in range(UNITS):
        inner, outer = inner_ref[slot], outer_ref[slot]
        below_ref[slot] = jnp.where(odd, inner, outer)
        above_ref[slot] = jnp.where(odd, outer, inner)
    spread_ref[...] = jnp.zeros(spread_ref.shape, jnp.float32)
    sides = (
        (below_ref, down_ref, DOWN_SLOT, UP),
        (down_ref, below_ref, UP_SLOT, range(len(DIRS))),
        (up_ref, above_ref, DOWN_SLOT, range(len(DIRS))),
        (above_ref, up_ref, UP_SLOT, DOWN),
    )
    for plane, (near, other, slots, wanted) in enumerate(sides):
        for tile in range(3):
            rows = slice(8 * tile, 8 * tile + 8)
            state = {i: other[slot, rows] for i, slot in slots.items()}
            total = add_moments([near[MOMENTS + part, rows] for part in range(4)], state)
            if plane in (1, 2):
                state.update({i: passed_ref[plane - 1, i, rows] for i in range(len(DIRS)) if i not in slots})
            out = relax(total, state, near[FLAG, rows] > 0.5, wanted)
            for i in wanted:
                relaxed_ref[plane, i, rows] = out[i]
    for plane in range(2):
        total = None
        for i, direction in enumerate(DIRS):
            value = shifted(relaxed_ref[plane + 1 - direction[2], i], direction)
            final_ref[i, plane] = value[0:16]
            total = add_moments(total, {i: value})
        inverse = 1.0 / total[0]
        velocity = [part * inverse for part in total[1:]]
        scalar = SPEED_GAIN * (velocity[0] * velocity[0] + velocity[1] * velocity[1] + velocity[2] * velocity[2])
        spread_ref[24 * plane : 24 * plane + 24, 0:128] = scalar
        spread_ref[64 + 24 * plane : 64 + 24 * plane + 24, 128:256] = scalar
    send_ref[...] = lax.dot_general(
        table_ref[...],
        spread_ref[...],
        (((1,), (1,)), ((), ())),
        precision=lax.Precision.HIGHEST,
        preferred_element_type=jnp.float32,
    )


def render_kernel(total_planes, got_ref, table_ref, part_ref):
    groups = part_ref.shape[0]
    samples = jnp.dot(
        got_ref[...], table_ref[...], precision=lax.Precision.HIGHEST, preferred_element_type=jnp.float32
    )
    depth = jnp.zeros((groups, 128), jnp.float32)
    light = [jnp.zeros((groups, 128), jnp.float32) for _ in range(3)]
    for source in range(got_ref.shape[0] // groups):
        for plane in range(2):
            sample = samples[groups * source : groups * (source + 1), 128 * plane : 128 * plane + 128]
            squared = sample * sample
            green = 1.0 / (1.0 + squared)
            saturation = squared * green
            extinction = (OPTICAL / total_planes) * saturation
            opacity = extinction * (
                1.0 - extinction * (0.5 - extinction * (1.0 / 6.0 - extinction * (1.0 / 24.0)))
            )
            blue = jnp.exp(-0.5 * (sample - 1.0) * (sample - 1.0))
            weight = jnp.exp(-depth) * opacity
            light[0] = light[0] + weight * saturation
            light[1] = light[1] + weight * green
            light[2] = light[2] + weight * blue
            depth = depth + extinction
    for channel, value in enumerate(light + [depth]):
        part_ref[:, channel, :] = value


def compose_kernel(got_ref, image_ref):
    ahead = jnp.zeros((1, 128), jnp.float32)
    light = jnp.zeros((4, 128), jnp.float32)
    for group in range(got_ref.shape[0]):
        part = got_ref[group]
        light = light + jnp.exp(-ahead) * part
        ahead = ahead + part[3:4]
    for channel in range(4):
        value = light[channel : channel + 1] if channel < 3 else 1.0 - jnp.exp(-ahead)
        image_ref[channel, 0:1, :] = value[:, 0:64]
        image_ref[channel, 1:2, :] = value[:, 64:128]


def cubic_weights(row):
    t = (row % 4 + 0.5) / 4.0
    return (
        (-(t**3) + 2.0 * t**2 - t) / 2.0,
        (3.0 * t**3 - 5.0 * t**2 + 2.0) / 2.0,
        (-3.0 * t**3 + 4.0 * t**2 + t) / 2.0,
        (t**3 - t**2) / 2.0,
    )


def x_table(nodes, group):
    table = np.zeros((2 * nodes, 2 * nodes), np.float32)
    for fine in range(4 * nodes):
        for offset, weight in zip((-1, 0, 1, 2), cubic_weights(fine - 2)):
            table[fine // 2, (fine % 2) * nodes + ((fine - 2) // 4 + offset) % nodes] += weight
    return table.reshape(-1, group, 2 * nodes).transpose(1, 0, 2).reshape(2 * nodes, 2 * nodes)


def y_table(rows):
    held = rows + 2 * HALO
    table = np.zeros((128, 256), np.float32)
    for fine in range(4 * rows):
        for offset, weight in zip((-1, 0, 1, 2), cubic_weights(fine - 2)):
            for column in range(2):
                for plane in range(2):
                    source = 64 * column + held * plane + ((fine - 2) // 4 + offset) % held
                    table[source, 128 * plane + 4 * rows * column + fine] += weight
    return table


def call(kernel, outs, scratch=(), spaces=None):
    vmem = pl.BlockSpec(memory_space=pltpu.VMEM)

    def run(*operands):
        shapes = [jax.ShapeDtypeStruct(shape, jnp.float32) for shape in outs]
        return pl.pallas_call(
            kernel,
            out_shape=shapes,
            in_specs=[pl.BlockSpec(memory_space=space) for space in spaces] if spaces else [vmem] * len(operands),
            out_specs=[vmem] * len(outs),
            scratch_shapes=[pltpu.VMEM(part, jnp.float32) if isinstance(part, tuple) else part for part in scratch],
            compiler_params=pltpu.CompilerParams(vmem_limit_bytes=VMEM_BYTES),
        )(*operands)

    return run


def body(populations, wall_flags):
    slabs = lax.axis_size("slab")
    dirs, planes, rows, nodes = populations.shape
    held = rows + 2 * HALO
    (edge,) = call(
        edge_kernel,
        [(dirs + 1, planes, 8, nodes)],
        scratch=[
            populations.shape,
            pltpu.VMEM(wall_flags.shape, jnp.int32),
            pltpu.SemaphoreType.DMA((2,)),
        ],
        spaces=[pltpu.HBM] * 2,
    )(*(pltpu.with_memory_space_constraint(part, pltpu.HBM) for part in (populations, wall_flags)))
    edge = lax.ppermute(edge, "col", [(0, 1), (1, 0)])
    odd = (lax.axis_index("slab") % 2).astype(jnp.int32).reshape(1)
    message = (UNITS, held, nodes)
    lattice = (2, dirs, held, nodes)
    passed, up, down, inner, outer = call(
        first_kernel, [lattice] + [message] * 4, scratch=[lattice], spaces=[pltpu.SMEM] + [pltpu.VMEM] * 3
    )(odd, populations, wall_flags, edge)
    outer = lax.ppermute(outer, "slab", [(i, (i + (1 if i % 2 else -1)) % slabs) for i in range(slabs)])
    inner = lax.ppermute(inner, "slab", [(i, i ^ 1) for i in range(slabs)])
    final, send = call(
        second_kernel,
        [populations.shape, (slabs, 128)],
        scratch=[message, message, (4, dirs, held, nodes), (128, 256)],
        spaces=[pltpu.SMEM] + [pltpu.VMEM] * 6,
    )(odd, passed, up, down, inner, outer, jnp.asarray(x_table(nodes, GROUP)))
    count = slabs // GROUP
    near = [[g * GROUP + i for i in range(GROUP)] for g in range(count)]
    far = [[g * GROUP + i for g in range(count)] for i in range(GROUP)]
    got = lax.all_to_all(send, "slab", 0, 0, axis_index_groups=near, tiled=True)
    (part,) = call(functools.partial(render_kernel, planes * slabs), [(count, 4, 128)])(got, jnp.asarray(y_table(rows)))
    got = lax.all_to_all(part, "slab", 0, 0, axis_index_groups=far, tiled=True)
    (image,) = call(compose_kernel, [(4, 2, 4 * rows)])(got)
    return jnp.transpose(image, (0, 2, 1)), final


def solution(mesh):
    return jax.shard_map(
        body,
        mesh=mesh,
        in_specs=(P(None, "slab", "col", None), P("slab", "col", None)),
        out_specs=(P(None, "col", "slab"), P(None, "slab", "col", None)),
        check_vma=False,
    )
```

```python
import functools

import jax
import jax.numpy as jnp
import numpy as np
from jax import lax
from jax.experimental import pallas as pl
from jax.experimental.pallas import tpu as pltpu
from jax.sharding import PartitionSpec as P

DIRS = (
    (0, 0, 0),
    (0, 0, 1), (1, 0, 1), (-1, 0, 1), (0, 1, 1), (0, -1, 1),
    (0, 0, -1), (1, 0, -1), (-1, 0, -1), (0, 1, -1), (0, -1, -1),
    (1, 0, 0), (-1, 0, 0), (0, 1, 0), (0, -1, 0),
    (1, 1, 0), (-1, -1, 0), (1, -1, 0), (-1, 1, 0),
)
OPP = tuple(DIRS.index(tuple(-e for e in d)) for d in DIRS)
WEIGHTS = tuple((1.0 / 3.0, 1.0 / 18.0, 1.0 / 36.0)[sum(abs(e) for e in d)] for d in DIRS)
UP = tuple(i for i, d in enumerate(DIRS) if d[2] == 1)
MID = tuple(i for i, d in enumerate(DIRS) if d[2] == 0)
DOWN = tuple(i for i, d in enumerate(DIRS) if d[2] == -1)
SPEED_GAIN = 10000.0
OPTICAL = 2.0

MOMENTS = len(UP)
FLAG = MOMENTS + 4
UNITS = FLAG + 1
UP_SLOT = {d: k for k, d in enumerate(UP)}
DOWN_SLOT = {d: k for k, d in enumerate(DOWN)}

VMEM_BYTES = 12 << 20
RUNS = 8
HALO = 4


def along(direction, vector):
    total = None
    for element, part in zip(direction, vector):
        if element:
            term = part if element > 0 else -part
            total = term if total is None else total + term
    return total


def add_moments(total, state):
    total = list(total) if total else [None] * 4
    for i, value in state.items():
        for part, element in enumerate((1,) + DIRS[i]):
            if element:
                held = total[part]
                if held is None:
                    total[part] = value if element > 0 else -value
                else:
                    total[part] = held + value if element > 0 else held - value
    return total


def relax(total, state, wall, wanted):
    density = total[0]
    inverse = 1.0 / density
    velocity = [part * inverse for part in total[1:]]
    speed_sq = velocity[0] * velocity[0] + velocity[1] * velocity[1] + velocity[2] * velocity[2]
    rest = 1.0 - 1.5 * speed_sq
    scaled = {w: w * density for w in sorted(set(WEIGHTS))}
    out = {}
    for i, direction in enumerate(DIRS):
        if i > OPP[i] or (i not in wanted and OPP[i] not in wanted):
            continue
        mass = scaled[WEIGHTS[i]]
        if i == 0:
            out[0] = jnp.where(wall, state[0], mass * rest)
            continue
        project = along(direction, velocity)
        even = rest + 4.5 * project * project
        odd = 3.0 * project
        if i in wanted:
            out[i] = jnp.where(wall, state[OPP[i]], mass * (even + odd))
        if OPP[i] in wanted:
            out[OPP[i]] = jnp.where(wall, state[i], mass * (even - odd))
    return out


def edge_kernel(pops_hbm, flags_hbm, edge_ref, pops_ref, flags_ref, sems):
    copies = [pltpu.make_async_copy(flags_hbm, flags_ref, sems.at[0])]
    for part in range(4):
        some = pl.ds(5 * part, min(5, len(DIRS) - 5 * part))
        copies.append(pltpu.make_async_copy(pops_hbm.at[some], pops_ref.at[some], sems.at[1 + part]))
    for copy in copies:
        copy.start()
    for copy in copies:
        copy.wait()
    lower = lax.broadcasted_iota(jnp.int32, (8, 128), 0) < HALO
    for plane in range(2):
        for i in range(len(DIRS)):
            edge_ref[i, plane] = jnp.where(lower, pops_ref[i, plane, 0:8], pops_ref[i, plane, 8:16])
        flags = jnp.where(lower, flags_ref[plane, 0:8], flags_ref[plane, 8:16])
        edge_ref[len(DIRS), plane] = flags.astype(jnp.float32)


def first_kernel(
    odd_ref, pops_ref, flags_ref, edge_ref,
    passed_ref, up_ref, down_ref, inner_ref, outer_ref,
    relaxed_ref,
):
    for plane, near in ((0, down_ref), (1, up_ref)):
        for tile in range(3):
            rows = slice(8 * tile, 8 * tile + 8)
            if tile < 2:
                state = {i: pops_ref[i, plane, rows] for i in range(len(DIRS))}
                flags = flags_ref[plane, rows].astype(jnp.float32)
            else:
                state = {i: edge_ref[i, plane] for i in range(len(DIRS))}
                flags = edge_ref[len(DIRS), plane]
            out = relax(add_moments(None, state), state, flags > 0.5, range(len(DIRS)))
            for i, value in out.items():
                relaxed_ref[plane, i, rows] = value
            near[FLAG, rows] = flags
    for plane, near, slots, inward in ((0, down_ref, DOWN_SLOT, DOWN), (1, up_ref, UP_SLOT, UP)):
        total = None
        for i in MID + inward:
            value = shifted(relaxed_ref[plane if i in MID else 1 - plane, i], DIRS[i])
            passed_ref[plane, i] = value
            total = add_moments(total, {i: value})
        for part, value in enumerate(total):
            near[MOMENTS + part] = value
        for i, slot in slots.items():
            near[slot] = shifted(relaxed_ref[plane, i], DIRS[i])
    odd = jnp.full(up_ref.shape[1:], odd_ref[0]) == 1
    for slot in range(UNITS):
        up, down = up_ref[slot], down_ref[slot]
        inner_ref[slot] = jnp.where(odd, down, up)
        outer_ref[slot] = jnp.where(odd, up, down)


def shifted(value, direction):
    cx, cy, _ = direction
    if cy:
        value = pltpu.roll(value, cy % value.shape[0], 0)
    if cx:
        value = pltpu.roll(value, cx % value.shape[1], 1)
    return value


def second_kernel(
    odd_ref, passed_ref, up_ref, down_ref, inner_ref, outer_ref, table_ref,
    final_hbm, send_ref,
    below_ref, above_ref, relaxed_ref, spread_ref, final_ref, sems,
):
    odd = jnp.full(up_ref.shape[1:], odd_ref[0]) == 1
    for slot in range(UNITS):
        inner, outer = inner_ref[slot], outer_ref[slot]
        below_ref[slot] = jnp.where(odd, inner, outer)
        above_ref[slot] = jnp.where(odd, outer, inner)
    spread_ref[...] = jnp.zeros(spread_ref.shape, jnp.float32)
    sides = (
        (below_ref, down_ref, DOWN_SLOT, UP),
        (down_ref, below_ref, UP_SLOT, range(len(DIRS))),
        (up_ref, above_ref, DOWN_SLOT, range(len(DIRS))),
        (above_ref, up_ref, UP_SLOT, DOWN),
    )
    for plane, (near, other, slots, wanted) in enumerate(sides):
        for tile in range(3):
            rows = slice(8 * tile, 8 * tile + 8)
            state = {i: other[slot, rows] for i, slot in slots.items()}
            total = add_moments([near[MOMENTS + part, rows] for part in range(4)], state)
            if plane in (1, 2):
                state.update({i: passed_ref[plane - 1, i, rows] for i in range(len(DIRS)) if i not in slots})
            out = relax(total, state, near[FLAG, rows] > 0.5, wanted)
            for i in wanted:
                relaxed_ref[plane, i, rows] = out[i]
    copies = []
    for plane in range(2):
        total = None
        for i, direction in enumerate(DIRS):
            value = shifted(relaxed_ref[plane + 1 - direction[2], i], direction)
            final_ref[plane, i] = value[0:16]
            total = add_moments(total, {i: value})
        copies.append(pltpu.make_async_copy(final_ref.at[plane], final_hbm.at[:, plane], sems.at[plane]))
        copies[-1].start()
        inverse = 1.0 / total[0]
        velocity = [part * inverse for part in total[1:]]
        scalar = SPEED_GAIN * (velocity[0] * velocity[0] + velocity[1] * velocity[1] + velocity[2] * velocity[2])
        spread_ref[24 * plane : 24 * plane + 24, 0:128] = scalar
        spread_ref[64 + 24 * plane : 64 + 24 * plane + 24, 128:256] = scalar
    send_ref[...] = lax.dot_general(
        table_ref[...],
        spread_ref[...],
        (((1,), (1,)), ((), ())),
        precision=lax.Precision.HIGHEST,
        preferred_element_type=jnp.float32,
    )
    for copy in copies:
        copy.wait()


def render_kernel(total_planes, got_ref, table_ref, image_ref):
    samples = jnp.dot(
        got_ref[...], table_ref[...], precision=lax.Precision.HIGHEST, preferred_element_type=jnp.float32
    )
    depth = jnp.zeros((RUNS, 128), jnp.float32)
    light = [jnp.zeros((RUNS, 128), jnp.float32) for _ in range(3)]
    for step in range(got_ref.shape[0] // RUNS):
        for plane in range(2):
            sample = samples[RUNS * step : RUNS * (step + 1), 128 * plane : 128 * plane + 128]
            squared = sample * sample
            green = 1.0 / (1.0 + squared)
            saturation = squared * green
            extinction = (OPTICAL / total_planes) * saturation
            opacity = extinction * (
                1.0 - extinction * (0.5 - extinction * (1.0 / 6.0 - extinction * (1.0 / 24.0)))
            )
            blue = jnp.exp(-0.5 * (sample - 1.0) * (sample - 1.0))
            weight = jnp.exp(-depth) * opacity
            light[0] = light[0] + weight * saturation
            light[1] = light[1] + weight * green
            light[2] = light[2] + weight * blue
            depth = depth + extinction
    row = lax.broadcasted_iota(jnp.int32, (RUNS, 128), 0)
    ahead = depth
    for step in (1, 2, 4):
        ahead = ahead + jnp.where(row >= step, pltpu.roll(ahead, step, 0), 0.0)
    through = jnp.exp(depth - ahead)
    sums = [jnp.sum(part * through, axis=0, keepdims=True) for part in light]
    sums.append(1.0 - jnp.exp(-jnp.sum(depth, axis=0, keepdims=True)))
    for channel, value in enumerate(sums):
        image_ref[channel, 0:1, :] = value[:, 0:64]
        image_ref[channel, 1:2, :] = value[:, 64:128]


def cubic_weights(row):
    t = (row % 4 + 0.5) / 4.0
    return (
        (-(t**3) + 2.0 * t**2 - t) / 2.0,
        (3.0 * t**3 - 5.0 * t**2 + 2.0) / 2.0,
        (-3.0 * t**3 + 4.0 * t**2 + t) / 2.0,
        (t**3 - t**2) / 2.0,
    )


def x_table(nodes, order):
    table = np.zeros((2 * nodes, 2 * nodes), np.float32)
    for fine in range(4 * nodes):
        for offset, weight in zip((-1, 0, 1, 2), cubic_weights(fine - 2)):
            table[fine // 2, (fine % 2) * nodes + ((fine - 2) // 4 + offset) % nodes] += weight
    return table[order]


def y_table(rows):
    held = rows + 2 * HALO
    table = np.zeros((128, 256), np.float32)
    for fine in range(4 * rows):
        for offset, weight in zip((-1, 0, 1, 2), cubic_weights(fine - 2)):
            for column in range(2):
                for plane in range(2):
                    source = 64 * column + held * plane + ((fine - 2) // 4 + offset) % held
                    table[source, 128 * plane + 4 * rows * column + fine] += weight
    return table


def call(kernel, outs, scratch=(), spaces=None, out_spaces=None):
    vmem = pl.BlockSpec(memory_space=pltpu.VMEM)

    def run(*operands):
        shapes = [jax.ShapeDtypeStruct(shape, jnp.float32) for shape in outs]
        return pl.pallas_call(
            kernel,
            out_shape=shapes,
            in_specs=[pl.BlockSpec(memory_space=space) for space in spaces] if spaces else [vmem] * len(operands),
            out_specs=[pl.BlockSpec(memory_space=space) for space in out_spaces] if out_spaces else [vmem] * len(outs),
            scratch_shapes=[pltpu.VMEM(part, jnp.float32) if isinstance(part, tuple) else part for part in scratch],
            compiler_params=pltpu.CompilerParams(vmem_limit_bytes=VMEM_BYTES),
        )(*operands)

    return run


def body(populations, wall_flags):
    slabs = lax.axis_size("slab")
    dirs, planes, rows, nodes = populations.shape
    held = rows + 2 * HALO
    order = [(slabs // RUNS) * (row % RUNS) + row // RUNS for row in range(slabs)]
    (edge,) = call(
        edge_kernel,
        [(dirs + 1, planes, 8, nodes)],
        scratch=[
            populations.shape,
            pltpu.VMEM(wall_flags.shape, jnp.int32),
            pltpu.SemaphoreType.DMA((5,)),
        ],
        spaces=[pltpu.HBM] * 2,
    )(*(pltpu.with_memory_space_constraint(part, pltpu.HBM) for part in (populations, wall_flags)))
    edge = lax.ppermute(edge, "col", [(0, 1), (1, 0)])
    odd = (lax.axis_index("slab") % 2).astype(jnp.int32).reshape(1)
    message = (UNITS, held, nodes)
    lattice = (2, dirs, held, nodes)
    passed, up, down, inner, outer = call(
        first_kernel, [lattice] + [message] * 4, scratch=[lattice], spaces=[pltpu.SMEM] + [pltpu.VMEM] * 3
    )(odd, populations, wall_flags, edge)
    outer = lax.ppermute(outer, "slab", [(i, (i + (1 if i % 2 else -1)) % slabs) for i in range(slabs)])
    inner = lax.ppermute(inner, "slab", [(i, i ^ 1) for i in range(slabs)])
    final, send = call(
        second_kernel,
        [populations.shape, (slabs, 128)],
        scratch=[
            message, message, (4, dirs, held, nodes), (128, 256), (2, dirs, rows, nodes),
            pltpu.SemaphoreType.DMA((2,)),
        ],
        spaces=[pltpu.SMEM] + [pltpu.VMEM] * 6,
        out_spaces=[pltpu.HBM, pltpu.VMEM],
    )(odd, passed, up, down, inner, outer, jnp.asarray(x_table(nodes, order)))
    got = lax.all_to_all(send, "slab", 0, 0, axis_index_groups=[order], tiled=True)
    (image,) = call(
        functools.partial(render_kernel, planes * slabs), [(4, 2, 4 * rows)]
    )(got, jnp.asarray(y_table(rows)))
    return jnp.transpose(image, (0, 2, 1)), final


def solution(mesh):
    return jax.shard_map(
        body,
        mesh=mesh,
        in_specs=(P(None, "slab", "col", None), P("slab", "col", None)),
        out_specs=(P(None, "col", "slab"), P(None, "slab", "col", None)),
        check_vma=False,
    )
```

```python
import functools

import jax
import jax.numpy as jnp
import numpy as np
from jax import lax
from jax.experimental import pallas as pl
from jax.experimental.pallas import tpu as pltpu
from jax.sharding import PartitionSpec as P

DIRS = (
    (0, 0, 0),
    (0, 0, 1), (1, 0, 1), (-1, 0, 1), (0, 1, 1), (0, -1, 1),
    (0, 0, -1), (1, 0, -1), (-1, 0, -1), (0, 1, -1), (0, -1, -1),
    (1, 0, 0), (-1, 0, 0), (0, 1, 0), (0, -1, 0),
    (1, 1, 0), (-1, -1, 0), (1, -1, 0), (-1, 1, 0),
)
OPP = tuple(DIRS.index(tuple(-e for e in d)) for d in DIRS)
WEIGHTS = tuple((1.0 / 3.0, 1.0 / 18.0, 1.0 / 36.0)[sum(abs(e) for e in d)] for d in DIRS)
UP = tuple(i for i, d in enumerate(DIRS) if d[2] == 1)
MID = tuple(i for i, d in enumerate(DIRS) if d[2] == 0)
DOWN = tuple(i for i, d in enumerate(DIRS) if d[2] == -1)
SPEED_GAIN = 10000.0
OPTICAL = 2.0

MOMENTS = len(UP)
FLAG = MOMENTS + 4
UNITS = FLAG + 1
UP_SLOT = {d: k for k, d in enumerate(UP)}
DOWN_SLOT = {d: k for k, d in enumerate(DOWN)}

VMEM_BYTES = 12 << 20
GROUP = 16
PLANE_ORDER = (8, 0, 9, 1, 10, 2, 11, 3, 12, 4, 13, 5, 14, 6, 15, 7)
HALO = 4


def along(direction, vector):
    total = None
    for element, part in zip(direction, vector):
        if element:
            term = part if element > 0 else -part
            total = term if total is None else total + term
    return total


def add_moments(total, state):
    total = list(total) if total else [None] * 4
    for i, value in state.items():
        for part, element in enumerate((1,) + DIRS[i]):
            if element:
                held = total[part]
                if held is None:
                    total[part] = value if element > 0 else -value
                else:
                    total[part] = held + value if element > 0 else held - value
    return total


def relax(total, state, wall, wanted):
    density = total[0]
    inverse = 1.0 / density
    velocity = [part * inverse for part in total[1:]]
    speed_sq = velocity[0] * velocity[0] + velocity[1] * velocity[1] + velocity[2] * velocity[2]
    rest = 1.0 - 1.5 * speed_sq
    scaled = {w: w * density for w in sorted(set(WEIGHTS))}
    out = {}
    for i, direction in enumerate(DIRS):
        if i > OPP[i] or (i not in wanted and OPP[i] not in wanted):
            continue
        mass = scaled[WEIGHTS[i]]
        if i == 0:
            out[0] = jnp.where(wall, state[0], mass * rest)
            continue
        project = along(direction, velocity)
        even = rest + 4.5 * project * project
        odd = 3.0 * project
        if i in wanted:
            out[i] = jnp.where(wall, state[OPP[i]], mass * (even + odd))
        if OPP[i] in wanted:
            out[OPP[i]] = jnp.where(wall, state[i], mass * (even - odd))
    return out


def edge_kernel(pops_hbm, flags_hbm, edge_ref, pops_ref, flags_ref, sems):
    copies = [pltpu.make_async_copy(flags_hbm, flags_ref, sems.at[0])]
    for part in range(4):
        some = pl.ds(5 * part, min(5, len(DIRS) - 5 * part))
        copies.append(pltpu.make_async_copy(pops_hbm.at[some], pops_ref.at[some], sems.at[1 + part]))
    for copy in copies:
        copy.start()
    for copy in copies:
        copy.wait()
    lower = lax.broadcasted_iota(jnp.int32, (8, 128), 0) < HALO
    for plane in range(2):
        for i in range(len(DIRS)):
            edge_ref[i, plane] = jnp.where(lower, pops_ref[i, plane, 0:8], pops_ref[i, plane, 8:16])
        flags = jnp.where(lower, flags_ref[plane, 0:8], flags_ref[plane, 8:16])
        edge_ref[len(DIRS), plane] = flags.astype(jnp.float32)


def first_kernel(
    odd_ref, pops_ref, flags_ref, edge_ref,
    passed_ref, up_ref, down_ref, inner_ref, outer_ref,
    relaxed_ref,
):
    for plane, near in ((0, down_ref), (1, up_ref)):
        for tile in range(3):
            rows = slice(8 * tile, 8 * tile + 8)
            if tile < 2:
                state = {i: pops_ref[i, plane, rows] for i in range(len(DIRS))}
                flags = flags_ref[plane, rows].astype(jnp.float32)
            else:
                state = {i: edge_ref[i, plane] for i in range(len(DIRS))}
                flags = edge_ref[len(DIRS), plane]
            out = relax(add_moments(None, state), state, flags > 0.5, range(len(DIRS)))
            for i, value in out.items():
                relaxed_ref[plane, i, rows] = value
            near[FLAG, rows] = flags
    for plane, near, slots, inward in ((0, down_ref, DOWN_SLOT, DOWN), (1, up_ref, UP_SLOT, UP)):
        total = None
        for i in MID + inward:
            value = shifted(relaxed_ref[plane if i in MID else 1 - plane, i], DIRS[i])
            passed_ref[plane, i] = value
            total = add_moments(total, {i: value})
        for part, value in enumerate(total):
            near[MOMENTS + part] = value
        for i, slot in slots.items():
            near[slot] = shifted(relaxed_ref[plane, i], DIRS[i])
    odd = jnp.full(up_ref.shape[1:], odd_ref[0]) == 1
    for slot in range(UNITS):
        up, down = up_ref[slot], down_ref[slot]
        inner_ref[slot] = jnp.where(odd, down, up)
        outer_ref[slot] = jnp.where(odd, up, down)


def shifted(value, direction):
    cx, cy, _ = direction
    if cy:
        value = pltpu.roll(value, cy % value.shape[0], 0)
    if cx:
        value = pltpu.roll(value, cx % value.shape[1], 1)
    return value


def second_kernel(
    odd_ref, passed_ref, up_ref, down_ref, inner_ref, outer_ref, table_ref,
    final_hbm, send_ref,
    below_ref, above_ref, relaxed_ref, spread_ref, final_ref, sems,
):
    odd = jnp.full(up_ref.shape[1:], odd_ref[0]) == 1
    for slot in range(UNITS):
        inner, outer = inner_ref[slot], outer_ref[slot]
        below_ref[slot] = jnp.where(odd, inner, outer)
        above_ref[slot] = jnp.where(odd, outer, inner)
    spread_ref[...] = jnp.zeros(spread_ref.shape, jnp.float32)
    sides = (
        (below_ref, down_ref, DOWN_SLOT, UP),
        (down_ref, below_ref, UP_SLOT, range(len(DIRS))),
        (up_ref, above_ref, DOWN_SLOT, range(len(DIRS))),
        (above_ref, up_ref, UP_SLOT, DOWN),
    )
    for plane, (near, other, slots, wanted) in enumerate(sides):
        for tile in range(3):
            rows = slice(8 * tile, 8 * tile + 8)
            state = {i: other[slot, rows] for i, slot in slots.items()}
            total = add_moments([near[MOMENTS + part, rows] for part in range(4)], state)
            if plane in (1, 2):
                state.update({i: passed_ref[plane - 1, i, rows] for i in range(len(DIRS)) if i not in slots})
            out = relax(total, state, near[FLAG, rows] > 0.5, wanted)
            for i in wanted:
                relaxed_ref[plane, i, rows] = out[i]
    copies = []
    for plane in range(2):
        total = None
        for i, direction in enumerate(DIRS):
            value = shifted(relaxed_ref[plane + 1 - direction[2], i], direction)
            final_ref[plane, i] = value[0:16]
            total = add_moments(total, {i: value})
        copies.append(pltpu.make_async_copy(final_ref.at[plane], final_hbm.at[:, plane], sems.at[plane]))
        copies[-1].start()
        inverse = 1.0 / total[0]
        velocity = [part * inverse for part in total[1:]]
        scalar = SPEED_GAIN * (velocity[0] * velocity[0] + velocity[1] * velocity[1] + velocity[2] * velocity[2])
        spread_ref[24 * plane : 24 * plane + 24, 0:128] = scalar
        spread_ref[64 + 24 * plane : 64 + 24 * plane + 24, 128:256] = scalar
    send_ref[...] = lax.dot_general(
        table_ref[...],
        spread_ref[...],
        (((1,), (1,)), ((), ())),
        precision=lax.Precision.HIGHEST,
        preferred_element_type=jnp.float32,
    )
    for copy in copies:
        copy.wait()


def render_kernel(total_planes, order, got_ref, table_ref, image_ref):
    runs = len(order)
    steps = got_ref.shape[0] // runs
    ordered = jnp.concatenate([got_ref[pl.ds(i, runs, stride=steps), :] for i in range(steps)], axis=0)
    samples = jnp.dot(
        ordered, table_ref[...], precision=lax.Precision.HIGHEST, preferred_element_type=jnp.float32
    )
    depth = jnp.zeros((runs, 128), jnp.float32)
    light = [jnp.zeros((runs, 128), jnp.float32) for _ in range(3)]
    for step in range(steps):
        sample = samples[runs * step : runs * (step + 1)]
        squared = sample * sample
        green = 1.0 / (1.0 + squared)
        saturation = squared * green
        extinction = (OPTICAL / total_planes) * saturation
        opacity = extinction * (1.0 - extinction * (0.5 - extinction * (1.0 / 6.0 - extinction * (1.0 / 24.0))))
        blue = jnp.exp(-0.5 * (sample - 1.0) * (sample - 1.0))
        for plane in range(2):
            lanes = slice(128 * plane, 128 * plane + 128)
            weight = jnp.exp(-depth) * opacity[:, lanes]
            light[0] = light[0] + weight * saturation[:, lanes]
            light[1] = light[1] + weight * green[:, lanes]
            light[2] = light[2] + weight * blue[:, lanes]
            depth = depth + extinction[:, lanes]
    row = lax.broadcasted_iota(jnp.int32, (runs, 128), 0)
    place = jnp.zeros((runs, 128), jnp.int32)
    for k, plane in enumerate(order):
        place = jnp.where(row == k, plane, place)
    ahead = jnp.zeros((runs, 128), jnp.float32)
    for k, plane in enumerate(order):
        ahead = ahead + jnp.where(place > plane, depth[k : k + 1], 0.0)
    through = jnp.exp(-ahead)
    sums = [jnp.sum(part * through, axis=0, keepdims=True) for part in light]
    sums.append(1.0 - jnp.exp(-jnp.sum(depth, axis=0, keepdims=True)))
    for channel, value in enumerate(sums):
        image_ref[channel, 0:1, :] = value[:, 0:64]
        image_ref[channel, 1:2, :] = value[:, 64:128]


def cubic_weights(row):
    t = (row % 4 + 0.5) / 4.0
    return (
        (-(t**3) + 2.0 * t**2 - t) / 2.0,
        (3.0 * t**3 - 5.0 * t**2 + 2.0) / 2.0,
        (-3.0 * t**3 + 4.0 * t**2 + t) / 2.0,
        (t**3 - t**2) / 2.0,
    )


def x_table(nodes, order):
    table = np.zeros((2 * nodes, 2 * nodes), np.float32)
    for fine in range(4 * nodes):
        for offset, weight in zip((-1, 0, 1, 2), cubic_weights(fine - 2)):
            table[fine // 2, (fine % 2) * nodes + ((fine - 2) // 4 + offset) % nodes] += weight
    return table[order]


def y_table(rows):
    held = rows + 2 * HALO
    table = np.zeros((128, 256), np.float32)
    for fine in range(4 * rows):
        for offset, weight in zip((-1, 0, 1, 2), cubic_weights(fine - 2)):
            for column in range(2):
                for plane in range(2):
                    source = 64 * column + held * plane + ((fine - 2) // 4 + offset) % held
                    table[source, 128 * plane + 4 * rows * column + fine] += weight
    return table


def call(kernel, outs, scratch=(), spaces=None, out_spaces=None):
    vmem = pl.BlockSpec(memory_space=pltpu.VMEM)

    def run(*operands):
        shapes = [jax.ShapeDtypeStruct(shape, jnp.float32) for shape in outs]
        return pl.pallas_call(
            kernel,
            out_shape=shapes,
            in_specs=[pl.BlockSpec(memory_space=space) for space in spaces] if spaces else [vmem] * len(operands),
            out_specs=[pl.BlockSpec(memory_space=space) for space in out_spaces] if out_spaces else [vmem] * len(outs),
            scratch_shapes=[pltpu.VMEM(part, jnp.float32) if isinstance(part, tuple) else part for part in scratch],
            compiler_params=pltpu.CompilerParams(vmem_limit_bytes=VMEM_BYTES),
        )(*operands)

    return run


def body(populations, wall_flags):
    slabs = lax.axis_size("slab")
    dirs, planes, rows, nodes = populations.shape
    held = rows + 2 * HALO
    order = [GROUP * plane + i for plane in PLANE_ORDER for i in range(GROUP)]
    (edge,) = call(
        edge_kernel,
        [(dirs + 1, planes, 8, nodes)],
        scratch=[
            populations.shape,
            pltpu.VMEM(wall_flags.shape, jnp.int32),
            pltpu.SemaphoreType.DMA((5,)),
        ],
        spaces=[pltpu.HBM] * 2,
    )(*(pltpu.with_memory_space_constraint(part, pltpu.HBM) for part in (populations, wall_flags)))
    edge = lax.ppermute(edge, "col", [(0, 1), (1, 0)])
    odd = (lax.axis_index("slab") % 2).astype(jnp.int32).reshape(1)
    message = (UNITS, held, nodes)
    lattice = (2, dirs, held, nodes)
    passed, up, down, inner, outer = call(
        first_kernel, [lattice] + [message] * 4, scratch=[lattice], spaces=[pltpu.SMEM] + [pltpu.VMEM] * 3
    )(odd, populations, wall_flags, edge)
    outer = lax.ppermute(outer, "slab", [(i, (i + (1 if i % 2 else -1)) % slabs) for i in range(slabs)])
    inner = lax.ppermute(inner, "slab", [(i, i ^ 1) for i in range(slabs)])
    final, send = call(
        second_kernel,
        [populations.shape, (slabs, 128)],
        scratch=[
            message, message, (4, dirs, held, nodes), (128, 256), (2, dirs, rows, nodes),
            pltpu.SemaphoreType.DMA((2,)),
        ],
        spaces=[pltpu.SMEM] + [pltpu.VMEM] * 6,
        out_spaces=[pltpu.HBM, pltpu.VMEM],
    )(odd, passed, up, down, inner, outer, jnp.asarray(x_table(nodes, order)))
    got = lax.all_to_all(send, "slab", 0, 0, axis_index_groups=[order], tiled=True)
    (image,) = call(
        functools.partial(render_kernel, planes * slabs, PLANE_ORDER), [(4, 2, 4 * rows)]
    )(got, jnp.asarray(y_table(rows)))
    return jnp.transpose(image, (0, 2, 1)), final


def solution(mesh):
    return jax.shard_map(
        body,
        mesh=mesh,
        in_specs=(P(None, "slab", "col", None), P("slab", "col", None)),
        out_specs=(P(None, "col", "slab"), P(None, "slab", "col", None)),
        check_vma=False,
    )
```

```python
import functools

import jax
import jax.numpy as jnp
import numpy as np
from jax import lax
from jax.experimental import pallas as pl
from jax.experimental.pallas import tpu as pltpu
from jax.sharding import PartitionSpec as P

DIRS = (
    (0, 0, 0),
    (0, 0, 1), (1, 0, 1), (-1, 0, 1), (0, 1, 1), (0, -1, 1),
    (0, 0, -1), (1, 0, -1), (-1, 0, -1), (0, 1, -1), (0, -1, -1),
    (1, 0, 0), (-1, 0, 0), (0, 1, 0), (0, -1, 0),
    (1, 1, 0), (-1, -1, 0), (1, -1, 0), (-1, 1, 0),
)
OPP = tuple(DIRS.index(tuple(-e for e in d)) for d in DIRS)
WEIGHTS = tuple((1.0 / 3.0, 1.0 / 18.0, 1.0 / 36.0)[sum(abs(e) for e in d)] for d in DIRS)
UP = tuple(i for i, d in enumerate(DIRS) if d[2] == 1)
MID = tuple(i for i, d in enumerate(DIRS) if d[2] == 0)
DOWN = tuple(i for i, d in enumerate(DIRS) if d[2] == -1)
SPEED_GAIN = 10000.0
OPTICAL = 2.0

MOMENTS = len(UP)
FLAG = MOMENTS + 4
UNITS = FLAG + 1
UP_SLOT = {d: k for k, d in enumerate(UP)}
DOWN_SLOT = {d: k for k, d in enumerate(DOWN)}

VMEM_BYTES = 12 << 20
GROUP = 16
PLANE_ORDER = (10, 11, 12, 13, 14, 15, 0, 1, 2, 3, 4, 5, 6, 7, 8, 9)
FIRST = 11
HALO = 4


def along(direction, vector):
    total = None
    for element, part in zip(direction, vector):
        if element:
            term = part if element > 0 else -part
            total = term if total is None else total + term
    return total


def add_moments(total, state):
    total = list(total) if total else [None] * 4
    for i, value in state.items():
        for part, element in enumerate((1,) + DIRS[i]):
            if element:
                held = total[part]
                if held is None:
                    total[part] = value if element > 0 else -value
                else:
                    total[part] = held + value if element > 0 else held - value
    return total


def relax(total, state, wall, wanted):
    density = total[0]
    inverse = 1.0 / density
    velocity = [part * inverse for part in total[1:]]
    speed_sq = velocity[0] * velocity[0] + velocity[1] * velocity[1] + velocity[2] * velocity[2]
    rest = 1.0 - 1.5 * speed_sq
    scaled = {w: w * density for w in sorted(set(WEIGHTS))}
    out = {}
    for i, direction in enumerate(DIRS):
        if i > OPP[i] or (i not in wanted and OPP[i] not in wanted):
            continue
        mass = scaled[WEIGHTS[i]]
        if i == 0:
            out[0] = jnp.where(wall, state[0], mass * rest)
            continue
        project = along(direction, velocity)
        even = rest + 4.5 * project * project
        odd = 3.0 * project
        if i in wanted:
            out[i] = jnp.where(wall, state[OPP[i]], mass * (even + odd))
        if OPP[i] in wanted:
            out[OPP[i]] = jnp.where(wall, state[i], mass * (even - odd))
    return out


def edge_kernel(pops_hbm, flags_hbm, edge_ref, pops_ref, flags_ref, sems):
    copies = [pltpu.make_async_copy(flags_hbm, flags_ref, sems.at[0])]
    for part in range(4):
        some = pl.ds(5 * part, min(5, len(DIRS) - 5 * part))
        copies.append(pltpu.make_async_copy(pops_hbm.at[some], pops_ref.at[some], sems.at[1 + part]))
    for copy in copies:
        copy.start()
    for copy in copies:
        copy.wait()
    lower = lax.broadcasted_iota(jnp.int32, (8, 128), 0) < HALO
    for plane in range(2):
        for i in range(len(DIRS)):
            edge_ref[i, plane] = jnp.where(lower, pops_ref[i, plane, 0:8], pops_ref[i, plane, 8:16])
        flags = jnp.where(lower, flags_ref[plane, 0:8], flags_ref[plane, 8:16])
        edge_ref[len(DIRS), plane] = flags.astype(jnp.float32)


def first_kernel(
    odd_ref, pops_ref, flags_ref, edge_ref,
    passed_ref, up_ref, down_ref, inner_ref, outer_ref,
    relaxed_ref,
):
    for plane, near in ((0, down_ref), (1, up_ref)):
        for tile in range(3):
            rows = slice(8 * tile, 8 * tile + 8)
            if tile < 2:
                state = {i: pops_ref[i, plane, rows] for i in range(len(DIRS))}
                flags = flags_ref[plane, rows].astype(jnp.float32)
            else:
                state = {i: edge_ref[i, plane] for i in range(len(DIRS))}
                flags = edge_ref[len(DIRS), plane]
            out = relax(add_moments(None, state), state, flags > 0.5, range(len(DIRS)))
            for i, value in out.items():
                relaxed_ref[plane, i, rows] = value
            near[FLAG, rows] = flags
    for plane, near, slots, inward in ((0, down_ref, DOWN_SLOT, DOWN), (1, up_ref, UP_SLOT, UP)):
        total = None
        for i in MID + inward:
            value = shifted(relaxed_ref[plane if i in MID else 1 - plane, i], DIRS[i])
            passed_ref[plane, i] = value
            total = add_moments(total, {i: value})
        for part, value in enumerate(total):
            near[MOMENTS + part] = value
        for i, slot in slots.items():
            near[slot] = shifted(relaxed_ref[plane, i], DIRS[i])
    odd = jnp.full(up_ref.shape[1:], odd_ref[0]) == 1
    for slot in range(UNITS):
        up, down = up_ref[slot], down_ref[slot]
        inner_ref[slot] = jnp.where(odd, down, up)
        outer_ref[slot] = jnp.where(odd, up, down)


def shifted(value, direction):
    cx, cy, _ = direction
    if cy:
        value = pltpu.roll(value, cy % value.shape[0], 0)
    if cx:
        value = pltpu.roll(value, cx % value.shape[1], 1)
    return value


def second_kernel(
    odd_ref, passed_ref, up_ref, down_ref, early_ref, late_ref, outer_ref, table_ref,
    final_hbm, send_ref,
    below_ref, above_ref, relaxed_ref, spread_ref, final_ref, sems,
):
    odd = jnp.full(up_ref.shape[1:], odd_ref[0]) == 1
    for slot in range(UNITS):
        inner, outer = early_ref[slot] + late_ref[slot], outer_ref[slot]
        below_ref[slot] = jnp.where(odd, inner, outer)
        above_ref[slot] = jnp.where(odd, outer, inner)
    spread_ref[...] = jnp.zeros(spread_ref.shape, jnp.float32)
    sides = (
        (below_ref, down_ref, DOWN_SLOT, UP),
        (down_ref, below_ref, UP_SLOT, range(len(DIRS))),
        (up_ref, above_ref, DOWN_SLOT, range(len(DIRS))),
        (above_ref, up_ref, UP_SLOT, DOWN),
    )
    for plane, (near, other, slots, wanted) in enumerate(sides):
        for tile in range(3):
            rows = slice(8 * tile, 8 * tile + 8)
            state = {i: other[slot, rows] for i, slot in slots.items()}
            total = add_moments([near[MOMENTS + part, rows] for part in range(4)], state)
            if plane in (1, 2):
                state.update({i: passed_ref[plane - 1, i, rows] for i in range(len(DIRS)) if i not in slots})
            out = relax(total, state, near[FLAG, rows] > 0.5, wanted)
            for i in wanted:
                relaxed_ref[plane, i, rows] = out[i]
    copies = []
    for plane in range(2):
        total = None
        for i, direction in enumerate(DIRS):
            value = shifted(relaxed_ref[plane + 1 - direction[2], i], direction)
            final_ref[plane, i] = value[0:16]
            total = add_moments(total, {i: value})
        copies.append(pltpu.make_async_copy(final_ref.at[plane], final_hbm.at[:, plane], sems.at[plane]))
        copies[-1].start()
        inverse = 1.0 / total[0]
        velocity = [part * inverse for part in total[1:]]
        scalar = SPEED_GAIN * (velocity[0] * velocity[0] + velocity[1] * velocity[1] + velocity[2] * velocity[2])
        spread_ref[24 * plane : 24 * plane + 24, 0:128] = scalar
        spread_ref[64 + 24 * plane : 64 + 24 * plane + 24, 128:256] = scalar
    send_ref[...] = lax.dot_general(
        table_ref[...],
        spread_ref[...],
        (((1,), (1,)), ((), ())),
        precision=lax.Precision.HIGHEST,
        preferred_element_type=jnp.float32,
    )
    for copy in copies:
        copy.wait()


def render_kernel(total_planes, order, got_ref, table_ref, image_ref):
    runs = len(order)
    steps = got_ref.shape[0] // runs
    ordered = jnp.concatenate(
        [got_ref[pl.ds((i - FIRST) % steps, runs, stride=steps), :] for i in range(steps)], axis=0
    )
    samples = jnp.dot(
        ordered, table_ref[...], precision=lax.Precision.HIGHEST, preferred_element_type=jnp.float32
    )
    depth = jnp.zeros((runs, 128), jnp.float32)
    light = [jnp.zeros((runs, 128), jnp.float32) for _ in range(3)]
    for step in range(steps):
        sample = samples[runs * step : runs * (step + 1)]
        squared = sample * sample
        green = 1.0 / (1.0 + squared)
        saturation = squared * green
        extinction = (OPTICAL / total_planes) * saturation
        opacity = extinction * (1.0 - extinction * (0.5 - extinction * (1.0 / 6.0 - extinction * (1.0 / 24.0))))
        blue = jnp.exp(-0.5 * (sample - 1.0) * (sample - 1.0))
        for plane in range(2):
            lanes = slice(128 * plane, 128 * plane + 128)
            weight = jnp.exp(-depth) * opacity[:, lanes]
            light[0] = light[0] + weight * saturation[:, lanes]
            light[1] = light[1] + weight * green[:, lanes]
            light[2] = light[2] + weight * blue[:, lanes]
            depth = depth + extinction[:, lanes]
    row = lax.broadcasted_iota(jnp.int32, (runs, 128), 0)
    place = jnp.zeros((runs, 128), jnp.int32)
    for k, plane in enumerate(order):
        place = jnp.where(row == k, plane, place)
    ahead = jnp.zeros((runs, 128), jnp.float32)
    for k, plane in enumerate(order):
        ahead = ahead + jnp.where(place > plane, depth[k : k + 1], 0.0)
    through = jnp.exp(-ahead)
    sums = [jnp.sum(part * through, axis=0, keepdims=True) for part in light]
    sums.append(1.0 - jnp.exp(-jnp.sum(depth, axis=0, keepdims=True)))
    for channel, value in enumerate(sums):
        image_ref[channel, 0:1, :] = value[:, 0:64]
        image_ref[channel, 1:2, :] = value[:, 64:128]


def cubic_weights(row):
    t = (row % 4 + 0.5) / 4.0
    return (
        (-(t**3) + 2.0 * t**2 - t) / 2.0,
        (3.0 * t**3 - 5.0 * t**2 + 2.0) / 2.0,
        (-3.0 * t**3 + 4.0 * t**2 + t) / 2.0,
        (t**3 - t**2) / 2.0,
    )


def x_table(nodes, order):
    table = np.zeros((2 * nodes, 2 * nodes), np.float32)
    for fine in range(4 * nodes):
        for offset, weight in zip((-1, 0, 1, 2), cubic_weights(fine - 2)):
            table[fine // 2, (fine % 2) * nodes + ((fine - 2) // 4 + offset) % nodes] += weight
    return table[order]


def y_table(rows):
    held = rows + 2 * HALO
    table = np.zeros((128, 256), np.float32)
    for fine in range(4 * rows):
        for offset, weight in zip((-1, 0, 1, 2), cubic_weights(fine - 2)):
            for column in range(2):
                for plane in range(2):
                    source = 64 * column + held * plane + ((fine - 2) // 4 + offset) % held
                    table[source, 128 * plane + 4 * rows * column + fine] += weight
    return table


def call(kernel, outs, scratch=(), spaces=None, out_spaces=None):
    vmem = pl.BlockSpec(memory_space=pltpu.VMEM)

    def run(*operands):
        shapes = [jax.ShapeDtypeStruct(shape, jnp.float32) for shape in outs]
        return pl.pallas_call(
            kernel,
            out_shape=shapes,
            in_specs=[pl.BlockSpec(memory_space=space) for space in spaces] if spaces else [vmem] * len(operands),
            out_specs=[pl.BlockSpec(memory_space=space) for space in out_spaces] if out_spaces else [vmem] * len(outs),
            scratch_shapes=[pltpu.VMEM(part, jnp.float32) if isinstance(part, tuple) else part for part in scratch],
            compiler_params=pltpu.CompilerParams(vmem_limit_bytes=VMEM_BYTES),
        )(*operands)

    return run


def body(populations, wall_flags):
    slabs = lax.axis_size("slab")
    dirs, planes, rows, nodes = populations.shape
    held = rows + 2 * HALO
    order = [GROUP * plane + (FIRST + i) % GROUP for plane in PLANE_ORDER for i in range(GROUP)]
    (edge,) = call(
        edge_kernel,
        [(dirs + 1, planes, 8, nodes)],
        scratch=[
            populations.shape,
            pltpu.VMEM(wall_flags.shape, jnp.int32),
            pltpu.SemaphoreType.DMA((5,)),
        ],
        spaces=[pltpu.HBM] * 2,
    )(*(pltpu.with_memory_space_constraint(part, pltpu.HBM) for part in (populations, wall_flags)))
    edge = lax.ppermute(edge, "col", [(0, 1), (1, 0)])
    odd = (lax.axis_index("slab") % 2).astype(jnp.int32).reshape(1)
    message = (UNITS, held, nodes)
    lattice = (2, dirs, held, nodes)
    passed, up, down, inner, outer = call(
        first_kernel, [lattice] + [message] * 4, scratch=[lattice], spaces=[pltpu.SMEM] + [pltpu.VMEM] * 3
    )(odd, populations, wall_flags, edge)
    halves = [[(i, i ^ 1) for i in range(slabs) if i // 2 % 2 == half] for half in range(2)]
    early = lax.ppermute(inner, "slab", halves[0])
    outer = lax.ppermute(outer, "slab", [(i, (i + (1 if i % 2 else -1)) % slabs) for i in range(slabs)])
    late = lax.ppermute(inner, "slab", halves[1])
    final, send = call(
        second_kernel,
        [populations.shape, (slabs, 128)],
        scratch=[
            message, message, (4, dirs, held, nodes), (128, 256), (2, dirs, rows, nodes),
            pltpu.SemaphoreType.DMA((2,)),
        ],
        spaces=[pltpu.SMEM] + [pltpu.VMEM] * 7,
        out_spaces=[pltpu.HBM, pltpu.VMEM],
    )(odd, passed, up, down, early, late, outer, jnp.asarray(x_table(nodes, order)))
    got = lax.all_to_all(send, "slab", 0, 0, axis_index_groups=[order], tiled=True)
    (image,) = call(
        functools.partial(render_kernel, planes * slabs, PLANE_ORDER), [(4, 2, 4 * rows)]
    )(got, jnp.asarray(y_table(rows)))
    return jnp.transpose(image, (0, 2, 1)), final


def solution(mesh):
    return jax.shard_map(
        body,
        mesh=mesh,
        in_specs=(P(None, "slab", "col", None), P("slab", "col", None)),
        out_specs=(P(None, "col", "slab"), P(None, "slab", "col", None)),
        check_vma=False,
    )
```

```python
import functools

import jax
import jax.numpy as jnp
import numpy as np
from jax import lax
from jax.experimental import pallas as pl
from jax.experimental.pallas import tpu as pltpu
from jax.sharding import PartitionSpec as P

DIRS = (
    (0, 0, 0),
    (0, 0, 1), (1, 0, 1), (-1, 0, 1), (0, 1, 1), (0, -1, 1),
    (0, 0, -1), (1, 0, -1), (-1, 0, -1), (0, 1, -1), (0, -1, -1),
    (1, 0, 0), (-1, 0, 0), (0, 1, 0), (0, -1, 0),
    (1, 1, 0), (-1, -1, 0), (1, -1, 0), (-1, 1, 0),
)
OPP = tuple(DIRS.index(tuple(-e for e in d)) for d in DIRS)
WEIGHTS = tuple((1.0 / 3.0, 1.0 / 18.0, 1.0 / 36.0)[sum(abs(e) for e in d)] for d in DIRS)
UP = tuple(i for i, d in enumerate(DIRS) if d[2] == 1)
MID = tuple(i for i, d in enumerate(DIRS) if d[2] == 0)
DOWN = tuple(i for i, d in enumerate(DIRS) if d[2] == -1)
SPEED_GAIN = 10000.0
OPTICAL = 2.0

MOMENTS = len(UP)
FLAG = MOMENTS + 4
UNITS = FLAG + 1
UP_SLOT = {d: k for k, d in enumerate(UP)}
DOWN_SLOT = {d: k for k, d in enumerate(DOWN)}

VMEM_BYTES = 12 << 20
GROUP = 16
PLANE_ORDER = (10, 11, 12, 13, 14, 15, 0, 1, 2, 3, 4, 5, 6, 7, 8, 9)
FIRST = 11
HALO = 4


def along(direction, vector):
    total = None
    for element, part in zip(direction, vector):
        if element:
            term = part if element > 0 else -part
            total = term if total is None else total + term
    return total


def add_moments(total, state):
    total = list(total) if total else [None] * 4
    for i, value in state.items():
        for part, element in enumerate((1,) + DIRS[i]):
            if element:
                held = total[part]
                if held is None:
                    total[part] = value if element > 0 else -value
                else:
                    total[part] = held + value if element > 0 else held - value
    return total


def relax(total, state, wall, wanted):
    density = total[0]
    inverse = 1.0 / density
    velocity = [part * inverse for part in total[1:]]
    speed_sq = velocity[0] * velocity[0] + velocity[1] * velocity[1] + velocity[2] * velocity[2]
    rest = 1.0 - 1.5 * speed_sq
    scaled = {w: w * density for w in sorted(set(WEIGHTS))}
    out = {}
    for i, direction in enumerate(DIRS):
        if i > OPP[i] or (i not in wanted and OPP[i] not in wanted):
            continue
        mass = scaled[WEIGHTS[i]]
        if i == 0:
            out[0] = jnp.where(wall, state[0], mass * rest)
            continue
        project = along(direction, velocity)
        even = rest + 4.5 * project * project
        odd = 3.0 * project
        if i in wanted:
            out[i] = jnp.where(wall, state[OPP[i]], mass * (even + odd))
        if OPP[i] in wanted:
            out[OPP[i]] = jnp.where(wall, state[i], mass * (even - odd))
    return out


def edge_kernel(pops_hbm, flags_hbm, edge_ref, pops_ref, flags_ref, sems):
    copies = [pltpu.make_async_copy(flags_hbm, flags_ref, sems.at[0])]
    for part in range(4):
        some = pl.ds(5 * part, min(5, len(DIRS) - 5 * part))
        copies.append(pltpu.make_async_copy(pops_hbm.at[some], pops_ref.at[some], sems.at[1 + part]))
    for copy in copies:
        copy.start()
    for copy in copies:
        copy.wait()
    lower = lax.broadcasted_iota(jnp.int32, (8, 128), 0) < HALO
    for plane in range(2):
        for i in range(len(DIRS)):
            edge_ref[i, plane] = jnp.where(lower, pops_ref[i, plane, 0:8], pops_ref[i, plane, 8:16])
        flags = jnp.where(lower, flags_ref[plane, 0:8], flags_ref[plane, 8:16])
        edge_ref[len(DIRS), plane] = flags.astype(jnp.float32)


def first_kernel(
    odd_ref, pops_ref, flags_ref, edge_ref,
    passed_ref, up_ref, down_ref, inner_ref, outer_ref,
    relaxed_ref,
):
    for plane, near in ((0, down_ref), (1, up_ref)):
        for tile in range(3):
            rows = slice(8 * tile, 8 * tile + 8)
            if tile < 2:
                state = {i: pops_ref[i, plane, rows] for i in range(len(DIRS))}
                flags = flags_ref[plane, rows].astype(jnp.float32)
            else:
                state = {i: edge_ref[i, plane] for i in range(len(DIRS))}
                flags = edge_ref[len(DIRS), plane]
            out = relax(add_moments(None, state), state, flags > 0.5, range(len(DIRS)))
            for i, value in out.items():
                relaxed_ref[plane, i, rows] = value
            near[FLAG, rows] = flags
    for plane, near, slots, inward in ((0, down_ref, DOWN_SLOT, DOWN), (1, up_ref, UP_SLOT, UP)):
        total = None
        for i in MID + inward:
            value = shifted(relaxed_ref[plane if i in MID else 1 - plane, i], DIRS[i])
            passed_ref[plane, i] = value
            total = add_moments(total, {i: value})
        for part, value in enumerate(total):
            near[MOMENTS + part] = value
        for i, slot in slots.items():
            near[slot] = shifted(relaxed_ref[plane, i], DIRS[i])
    odd = jnp.full(up_ref.shape[1:], odd_ref[0]) == 1
    for slot in range(UNITS):
        up, down = up_ref[slot], down_ref[slot]
        inner_ref[slot] = jnp.where(odd, down, up)
        outer_ref[slot] = jnp.where(odd, up, down)


def shifted(value, direction):
    cx, cy, _ = direction
    if cy:
        value = pltpu.roll(value, cy % value.shape[0], 0)
    if cx:
        value = pltpu.roll(value, cx % value.shape[1], 1)
    return value


def second_kernel(
    odd_ref, passed_ref, up_ref, down_ref, early_ref, late_ref, outer_ref, table_ref,
    final_ref, send_ref,
    below_ref, above_ref, relaxed_ref, spread_ref,
):
    odd = jnp.full(up_ref.shape[1:], odd_ref[0]) == 1
    for slot in range(UNITS):
        inner, outer = early_ref[slot] + late_ref[slot], outer_ref[slot]
        below_ref[slot] = jnp.where(odd, inner, outer)
        above_ref[slot] = jnp.where(odd, outer, inner)
    spread_ref[...] = jnp.zeros(spread_ref.shape, jnp.float32)
    sides = (
        (below_ref, down_ref, DOWN_SLOT, UP),
        (down_ref, below_ref, UP_SLOT, range(len(DIRS))),
        (up_ref, above_ref, DOWN_SLOT, range(len(DIRS))),
        (above_ref, up_ref, UP_SLOT, DOWN),
    )
    for plane, (near, other, slots, wanted) in enumerate(sides):
        for tile in range(3):
            rows = slice(8 * tile, 8 * tile + 8)
            state = {i: other[slot, rows] for i, slot in slots.items()}
            total = add_moments([near[MOMENTS + part, rows] for part in range(4)], state)
            if plane in (1, 2):
                state.update({i: passed_ref[plane - 1, i, rows] for i in range(len(DIRS)) if i not in slots})
            out = relax(total, state, near[FLAG, rows] > 0.5, wanted)
            for i in wanted:
                relaxed_ref[plane, i, rows] = out[i]
    for plane in range(2):
        total = None
        for i, direction in enumerate(DIRS):
            value = shifted(relaxed_ref[plane + 1 - direction[2], i], direction)
            final_ref[plane, i] = value[0:16]
            total = add_moments(total, {i: value})
        inverse = 1.0 / total[0]
        velocity = [part * inverse for part in total[1:]]
        scalar = SPEED_GAIN * (velocity[0] * velocity[0] + velocity[1] * velocity[1] + velocity[2] * velocity[2])
        spread_ref[24 * plane : 24 * plane + 24, 0:128] = scalar
        spread_ref[64 + 24 * plane : 64 + 24 * plane + 24, 128:256] = scalar
    send_ref[...] = lax.dot_general(
        table_ref[...],
        spread_ref[...],
        (((1,), (1,)), ((), ())),
        precision=lax.Precision.HIGHEST,
        preferred_element_type=jnp.float32,
    )


def render_kernel(total_planes, order, got_ref, table_ref, final_ref, image_ref, final_hbm, sems):
    copies = [pltpu.make_async_copy(final_ref.at[plane], final_hbm.at[:, plane], sems.at[plane]) for plane in range(2)]
    for copy in copies:
        copy.start()
    runs = len(order)
    steps = got_ref.shape[0] // runs
    ordered = jnp.concatenate(
        [got_ref[pl.ds((i - FIRST) % steps, runs, stride=steps), :] for i in range(steps)], axis=0
    )
    samples = jnp.dot(
        ordered, table_ref[...], precision=lax.Precision.HIGHEST, preferred_element_type=jnp.float32
    )
    depth = jnp.zeros((runs, 128), jnp.float32)
    light = [jnp.zeros((runs, 128), jnp.float32) for _ in range(3)]
    for step in range(steps):
        sample = samples[runs * step : runs * (step + 1)]
        squared = sample * sample
        green = 1.0 / (1.0 + squared)
        saturation = squared * green
        extinction = (OPTICAL / total_planes) * saturation
        opacity = extinction * (1.0 - extinction * (0.5 - extinction * (1.0 / 6.0 - extinction * (1.0 / 24.0))))
        blue = jnp.exp(-0.5 * (sample - 1.0) * (sample - 1.0))
        for plane in range(2):
            lanes = slice(128 * plane, 128 * plane + 128)
            weight = jnp.exp(-depth) * opacity[:, lanes]
            light[0] = light[0] + weight * saturation[:, lanes]
            light[1] = light[1] + weight * green[:, lanes]
            light[2] = light[2] + weight * blue[:, lanes]
            depth = depth + extinction[:, lanes]
    row = lax.broadcasted_iota(jnp.int32, (runs, 128), 0)
    place = jnp.zeros((runs, 128), jnp.int32)
    for k, plane in enumerate(order):
        place = jnp.where(row == k, plane, place)
    ahead = jnp.zeros((runs, 128), jnp.float32)
    for k, plane in enumerate(order):
        ahead = ahead + jnp.where(place > plane, depth[k : k + 1], 0.0)
    through = jnp.exp(-ahead)
    sums = [jnp.sum(part * through, axis=0, keepdims=True) for part in light]
    sums.append(1.0 - jnp.exp(-jnp.sum(depth, axis=0, keepdims=True)))
    for channel, value in enumerate(sums):
        image_ref[channel, 0:1, :] = value[:, 0:64]
        image_ref[channel, 1:2, :] = value[:, 64:128]
    for copy in copies:
        copy.wait()


def cubic_weights(row):
    t = (row % 4 + 0.5) / 4.0
    return (
        (-(t**3) + 2.0 * t**2 - t) / 2.0,
        (3.0 * t**3 - 5.0 * t**2 + 2.0) / 2.0,
        (-3.0 * t**3 + 4.0 * t**2 + t) / 2.0,
        (t**3 - t**2) / 2.0,
    )


def x_table(nodes, order):
    table = np.zeros((2 * nodes, 2 * nodes), np.float32)
    for fine in range(4 * nodes):
        for offset, weight in zip((-1, 0, 1, 2), cubic_weights(fine - 2)):
            table[fine // 2, (fine % 2) * nodes + ((fine - 2) // 4 + offset) % nodes] += weight
    return table[order]


def y_table(rows):
    held = rows + 2 * HALO
    table = np.zeros((128, 256), np.float32)
    for fine in range(4 * rows):
        for offset, weight in zip((-1, 0, 1, 2), cubic_weights(fine - 2)):
            for column in range(2):
                for plane in range(2):
                    source = 64 * column + held * plane + ((fine - 2) // 4 + offset) % held
                    table[source, 128 * plane + 4 * rows * column + fine] += weight
    return table


def call(kernel, outs, scratch=(), spaces=None, out_spaces=None):
    vmem = pl.BlockSpec(memory_space=pltpu.VMEM)

    def run(*operands):
        shapes = [jax.ShapeDtypeStruct(shape, jnp.float32) for shape in outs]
        return pl.pallas_call(
            kernel,
            out_shape=shapes,
            in_specs=[pl.BlockSpec(memory_space=space) for space in spaces] if spaces else [vmem] * len(operands),
            out_specs=[pl.BlockSpec(memory_space=space) for space in out_spaces] if out_spaces else [vmem] * len(outs),
            scratch_shapes=[pltpu.VMEM(part, jnp.float32) if isinstance(part, tuple) else part for part in scratch],
            compiler_params=pltpu.CompilerParams(vmem_limit_bytes=VMEM_BYTES),
        )(*operands)

    return run


def body(populations, wall_flags):
    slabs = lax.axis_size("slab")
    dirs, planes, rows, nodes = populations.shape
    held = rows + 2 * HALO
    order = [GROUP * plane + (FIRST + i) % GROUP for plane in PLANE_ORDER for i in range(GROUP)]
    (edge,) = call(
        edge_kernel,
        [(dirs + 1, planes, 8, nodes)],
        scratch=[
            populations.shape,
            pltpu.VMEM(wall_flags.shape, jnp.int32),
            pltpu.SemaphoreType.DMA((5,)),
        ],
        spaces=[pltpu.HBM] * 2,
    )(*(pltpu.with_memory_space_constraint(part, pltpu.HBM) for part in (populations, wall_flags)))
    edge = lax.ppermute(edge, "col", [(0, 1), (1, 0)])
    odd = (lax.axis_index("slab") % 2).astype(jnp.int32).reshape(1)
    message = (UNITS, held, nodes)
    lattice = (2, dirs, held, nodes)
    passed, up, down, inner, outer = call(
        first_kernel, [lattice] + [message] * 4, scratch=[lattice], spaces=[pltpu.SMEM] + [pltpu.VMEM] * 3
    )(odd, populations, wall_flags, edge)
    halves = [[(i, i ^ 1) for i in range(slabs) if i // 2 % 2 == half] for half in range(2)]
    early = lax.ppermute(inner, "slab", halves[0])
    outer = lax.ppermute(outer, "slab", [(i, (i + (1 if i % 2 else -1)) % slabs) for i in range(slabs)])
    late = lax.ppermute(inner, "slab", halves[1])
    final, send = call(
        second_kernel,
        [(planes, dirs, rows, nodes), (slabs, 128)],
        scratch=[
            message, message, (4, dirs, held, nodes), (128, 256),
        ],
        spaces=[pltpu.SMEM] + [pltpu.VMEM] * 7,
    )(odd, passed, up, down, early, late, outer, jnp.asarray(x_table(nodes, order)))
    got = lax.all_to_all(send, "slab", 0, 0, axis_index_groups=[order], tiled=True)
    image, final = call(
        functools.partial(render_kernel, planes * slabs, PLANE_ORDER),
        [(4, 2, 4 * rows), populations.shape],
        scratch=[pltpu.SemaphoreType.DMA((2,))],
        out_spaces=[pltpu.VMEM, pltpu.HBM],
    )(got, jnp.asarray(y_table(rows)), final)
    return jnp.transpose(image, (0, 2, 1)), final


def solution(mesh):
    return jax.shard_map(
        body,
        mesh=mesh,
        in_specs=(P(None, "slab", "col", None), P("slab", "col", None)),
        out_specs=(P(None, "col", "slab"), P(None, "slab", "col", None)),
        check_vma=False,
    )
```
